32 devices in a mesh: seq: 4 (over z), head: 2 (over core), batch: 4 (over y, x).
Axes of the slice: x: 2, y: 2, z: 4, core: 2. Of those that a mesh axis runs over, the one named last changes fastest.
Arguments:
- tokens: bfloat16 [8, 4096, 1024], P('batch', 'seq'), may hold values from -6 to 6
- cotangent: bfloat16 [8, 4096, 1024], P('batch', 'seq'), may hold values from -6 to 6
- adapter_index: int32 [8], P('batch'), may hold values from 0 to 7
- norm_gain: float32 [1024], replicated, may hold values from 0.5 to 1.5
- gate_input_weight: bfloat16 [1024, 2, 2048], P(None, None, 'head'), may hold values from -0.1875 to 0.1875
- bc_weight: bfloat16 [1024, 2, 128], P(None, None, 'head'), may hold values from -0.1875 to 0.1875
- step_weight: bfloat16 [1024, 32], P(None, 'head'), may hold values from -0.1875 to 0.1875
- conv_x: float32 [5, 2048], P(None, 'head'), may hold values from -0.6 to 0.6
- conv_bc: float32 [5, 2, 128], P(None, None, 'head'), may hold values from -0.6 to 0.6
- dt_bias: float32 [32], P('head'), may hold values from -6 to -2
- a_log: float32 [32], P('head'), may hold values from -4.6 to 2
- skip_gain: float32 [32], P('head'), may hold values from 0.5 to 1.5
- out_gain: float32 [2048], P('head'), may hold values from 0.5 to 1.5
- output_weight: bfloat16 [2048, 1024], P('head'), may hold values from -0.125 to 0.125
- in_down: bfloat16 [8, 1024, 16], replicated, may hold values from -0.1875 to 0.1875
- in_up: bfloat16 [8, 16, 2, 2048], P(None, None, None, 'head'), may hold values from -0.8984375 to 0.8984375
- out_down: bfloat16 [8, 2048, 16], P(None, 'head'), may hold values from -0.125 to 0.125
- out_up: bfloat16 [8, 16, 1024], replicated, may hold values from -0.8984375 to 0.8984375
Outputs:
- result: bfloat16 [8, 4096, 1024], P('batch', 'seq', 'head')
- grad_tokens: bfloat16 [8, 4096, 1024], P('batch', 'seq', 'head')
- grad_in_down: float32 [8, 1024, 16], replicated
- grad_in_up: float32 [8, 16, 2, 2048], P(None, None, None, 'head')
- grad_out_down: float32 [8, 2048, 16], P(None, 'head')
- grad_out_up: float32 [8, 16, 1024], replicated
The draws below stay inside these ranges and needn't reach their ends.
All inputs are finite; a program needn't handle non-finite values.
Results may differ from the reference program's by a relative error of at most 0.0035.
The reference program's roundings to bfloat16 on the way count: a program that leaves them out, or rounds other values in their place, can miss the bound.
Values may be sent and summed in bfloat16 or wider, within the bound.
A program may use at most 256 MiB of HBM per device.

```python
import jax
import jax.numpy as jnp
from jax import lax

D = 1024
INNER = 2048
HEADS = 32
HEADDIM = 64
NSTATE = 128
KCONV = 4
STRETCH = 256
ADAPTERS = 8
RANK = 16
LENGTH = 4096
SEQS = 8


def set_ends(entries, stream_key, low, high):
    extent = entries.shape
    index_at = [jax.random.randint(jax.random.fold_in(stream_key, axis), (), 0, extent[axis]) for axis in range(len(extent))]
    entries = entries.at[tuple(index_at)].set(low)
    longest = extent.index(max(extent))
    index_at[longest] = (index_at[longest] + 1) % extent[longest]
    return entries.at[tuple(index_at)].set(high)


def level_of(rng, extent, shards, least, top_value):
    def one(dim, blocks):
        draws = jax.random.uniform(jax.random.fold_in(jax.random.fold_in(rng, 6), dim), (blocks,), jnp.float32, least / len(shards), top_value / len(shards))
        return jnp.repeat(jnp.exp(draws), extent[dim] // blocks).reshape((-1,) + (1,) * (len(extent) - dim - 1))

    factor_of = one(*shards[0])
    for cut in shards[1:]:
        factor_of = factor_of * one(*cut)
    return factor_of


def bell_draw(own_key, shape, width, reach, cuts=(), kind=jnp.bfloat16):
    factor_of = level_of(own_key, shape, cuts, -0.22, 0.18) if cuts else 1.0
    result = jax.random.normal(own_key, shape, jnp.float32) * width * factor_of
    return jnp.minimum(jnp.maximum(result, -reach), reach).astype(kind)


def setup_inputs(seed: int = 0) -> dict:
    streams_of = jax.random.split(jax.random.key(seed), 19)
    tokens = bell_draw(streams_of[0], (SEQS, LENGTH, D), 1.0, 6.0, ((0, 4), (1, 4)))
    cotangent = bell_draw(streams_of[1], (SEQS, LENGTH, D), 1.0, 6.0, ((0, 4), (1, 4)))
    adapter_index = set_ends(jax.random.randint(streams_of[2], (SEQS,), 0, ADAPTERS), jax.random.fold_in(streams_of[2], 1), 0, ADAPTERS - 1).astype(jnp.int32)
    norm_gain = jnp.clip(1.0 + 0.1 * jax.random.normal(streams_of[3], (D,), jnp.float32), 0.5, 1.5)
    gate_input_weight = bell_draw(streams_of[4], (D, 2, INNER), D ** -0.5, 0.1875, ((2, 2),))
    bc_weight = bell_draw(streams_of[5], (D, 2, NSTATE), D ** -0.5, 0.1875, ((2, 2),))
    step_weight = bell_draw(streams_of[6], (D, HEADS), D ** -0.5, 0.1875, ((1, 2),))
    conv_x = jnp.clip(jax.random.uniform(streams_of[7], (KCONV + 1, INNER), jnp.float32, -0.6, 0.6) * level_of(streams_of[7], (KCONV + 1, INNER), ((1, 2),), -0.4, 0.0), -0.6, 0.6)
    conv_bc = jnp.clip(jax.random.uniform(streams_of[8], (KCONV + 1, 2, NSTATE), jnp.float32, -0.6, 0.6) * level_of(streams_of[8], (KCONV + 1, 2, NSTATE), ((2, 2),), -0.4, 0.0), -0.6, 0.6)
    dt_bias = jnp.clip(-6.0 + 4.0 * jax.random.uniform(streams_of[9], (HEADS,), jnp.float32) ** level_of(streams_of[9], (HEADS,), ((0, 2),), -0.2, 0.2), -6.0, -2.0)
    a_log = jnp.clip(-4.6 + 6.6 * jax.random.uniform(streams_of[10], (HEADS,), jnp.float32) ** level_of(streams_of[10], (HEADS,), ((0, 2),), -0.2, 0.2), -4.6, 2.0)
    skip_gain = jnp.clip(0.5 + 1.0 * jax.random.uniform(streams_of[11], (HEADS,), jnp.float32) ** level_of(streams_of[11], (HEADS,), ((0, 2),), -0.2, 0.2), 0.5, 1.5)
    out_gain = jnp.clip(1.0 + 0.1 * jax.random.normal(streams_of[12], (INNER,), jnp.float32), 0.5, 1.5)
    output_weight = bell_draw(streams_of[13], (INNER, D), INNER ** -0.5, 0.125, ((0, 2),))
    in_down = bell_draw(streams_of[14], (ADAPTERS, D, RANK), D ** -0.5, 0.1875)
    in_up = bell_draw(streams_of[15], (ADAPTERS, RANK, 2, INNER), 0.15, 0.8984375, ((3, 2),))
    out_down = bell_draw(streams_of[16], (ADAPTERS, INNER, RANK), INNER ** -0.5, 0.125, ((1, 2),))
    out_up = bell_draw(streams_of[17], (ADAPTERS, RANK, D), 0.15, 0.8984375)
    return {"tokens": tokens, "cotangent": cotangent, "adapter_index": adapter_index, "norm_gain": norm_gain, "gate_input_weight": gate_input_weight, "bc_weight": bc_weight, "step_weight": step_weight, "conv_x": conv_x, "conv_bc": conv_bc, "dt_bias": dt_bias, "a_log": a_log, "skip_gain": skip_gain, "out_gain": out_gain, "output_weight": output_weight, "in_down": in_down, "in_up": in_up, "out_down": out_down, "out_up": out_up}


EPSILON = 1e-05
EXACT_MATMUL = lax.Precision.HIGHEST

@jax.custom_vjp
def low(v):
    return lax.optimization_barrier(v.astype(jnp.bfloat16)).astype(jnp.float32)

@jax.custom_vjp
def low_back(v):
    return v

def low_keep(v):
    return (low(v), None)

def low_pass(kept, grad):
    return (grad,)

def back_keep(v):
    return (v, None)

def back_low(kept, grad):
    return (low(grad),)
low.defvjp(low_keep, low_pass)
low_back.defvjp(back_keep, back_low)

def causal_conv(values, tap_table):
    tap_span = tap_table.shape[0] - 1
    length = values.shape[0]
    padded = jnp.concatenate([jnp.zeros((tap_span - 1,) + values.shape[1:], jnp.float32), values], 0)
    summed = tap_table[tap_span]
    for tap_index in range(tap_span):
        summed = summed + tap_table[tap_index] * padded[tap_index:tap_index + length]
    return summed

def scan_heads(head_input, b_val, c_val, step_size, log_decay):
    length = head_input.shape[0]
    block_len = min(STRETCH, length)
    block_count = length // block_len

    def one_block(carry_state, pieces):
        x_block, b_block, c_block, step_block, log_block = pieces
        running = jnp.cumsum(log_block, 0)
        places = jnp.arange(block_len)
        allowed = (places[:, None] >= places[None, :])[:, :, None]
        spread = jnp.where(allowed, running[:, None, :] - running[None, :, :], -jnp.inf)
        scores = jnp.dot(c_block, b_block.T, precision=EXACT_MATMUL)
        weights = jnp.exp(spread) * scores[:, :, None] * step_block[None, :, :]
        within = jnp.einsum('tsh,shp->thp', weights, x_block, precision=EXACT_MATMUL)
        carried = jnp.exp(running)[:, :, None] * jnp.einsum('tn,hpn->thp', c_block, carry_state, precision=EXACT_MATMUL)
        tail_weight = jnp.exp(running[-1:] - running) * step_block
        new_state = jnp.exp(running[-1])[:, None, None] * carry_state + jnp.einsum('sh,shp,sn->hpn', tail_weight, x_block, b_block, precision=EXACT_MATMUL)
        return (new_state, within + carried)
    initial = jnp.zeros((head_input.shape[1], head_input.shape[2], b_val.shape[1]), jnp.float32)
    pieces = tuple((v.reshape((block_count, block_len) + v.shape[1:]) for v in (head_input, b_val, c_val, step_size, log_decay)))
    _, scanned = lax.scan(jax.checkpoint(one_block), initial, pieces)
    return scanned.reshape(head_input.shape)

def layer(tokens_f, down_in, up_in, down_out, up_out, norm_gain, gate_input_weight, bc_weight, step_weight, conv_x, conv_bc, dt_bias, a_log, skip_gain, out_gain, output_weight):
    length = tokens_f.shape[0]
    normalized_rows = low(tokens_f * lax.rsqrt(lax.optimization_barrier(jnp.mean(tokens_f * tokens_f, -1, keepdims=True)) + EPSILON) * norm_gain)
    lowrank_product = jnp.dot(normalized_rows, down_in, precision=EXACT_MATMUL)
    projected_rows = jnp.einsum('ld,dki->lki', normalized_rows, gate_input_weight, precision=EXACT_MATMUL) + jnp.einsum('lr,rki->lki', lowrank_product, up_in, precision=EXACT_MATMUL)
    projected_rows = low(low_back(projected_rows))
    raw_bc_values = low(low_back(jnp.einsum('ld,dkn->lkn', normalized_rows, bc_weight, precision=EXACT_MATMUL)))
    raw_step_sizes = low(low_back(jnp.dot(normalized_rows, step_weight, precision=EXACT_MATMUL)))
    x_conv = low(jax.nn.silu(causal_conv(projected_rows[:, 1], conv_x)))
    bc_conv = low(jax.nn.silu(causal_conv(raw_bc_values, conv_bc)))
    step_size = jax.nn.softplus(raw_step_sizes + dt_bias)
    log_decay = step_size * -jnp.exp(a_log)
    head_input = x_conv.reshape(length, HEADS, HEADDIM)
    y_val = scan_heads(head_input, bc_conv[:, 0], bc_conv[:, 1], step_size, log_decay) + skip_gain[:, None] * head_input
    gated = y_val.reshape(length, INNER) * jax.nn.silu(projected_rows[:, 0])
    norm_output = low(gated * lax.rsqrt(lax.optimization_barrier(jnp.mean(gated * gated, -1, keepdims=True)) + EPSILON) * out_gain)
    mixed = jnp.dot(norm_output, output_weight, precision=EXACT_MATMUL) + jnp.dot(jnp.dot(norm_output, down_out, precision=EXACT_MATMUL), up_out, precision=EXACT_MATMUL)
    return tokens_f + mixed

def reference(tokens, cotangent, adapter_index, norm_gain, gate_input_weight, bc_weight, step_weight, conv_x, conv_bc, dt_bias, a_log, skip_gain, out_gain, output_weight, in_down, in_up, out_down, out_up):
    fixed_parts = tuple((v.astype(jnp.float32) for v in (norm_gain, gate_input_weight, bc_weight, step_weight, conv_x, conv_bc, dt_bias, a_log, skip_gain, out_gain, output_weight)))
    tables = tuple((v.astype(jnp.float32) for v in (in_down, in_up, out_down, out_up)))

    def per_sequence(totals, item):
        seq_tokens, seq_cot, index = item
        picked = tuple((table[index] for table in tables))

        def run(tokens_f, down_in, up_in, down_out, up_out):
            return layer(tokens_f, down_in, up_in, down_out, up_out, *fixed_parts)
        outputs, pull = jax.vjp(run, seq_tokens.astype(jnp.float32), *picked)
        grads = pull(seq_cot.astype(jnp.float32))
        totals = tuple((total.at[index].add(grad) for total, grad in zip(totals, grads[1:])))
        return (totals, (outputs.astype(jnp.bfloat16), grads[0].astype(jnp.bfloat16)))
    zero_tables = tuple((jnp.zeros(table.shape, jnp.float32) for table in tables))
    totals, (results, grad_tokens) = lax.scan(per_sequence, zero_tables, (tokens, cotangent, adapter_index))
    return (results, grad_tokens, totals[0], totals[1], totals[2], totals[3])
```

```python
import functools

import jax
import jax.numpy as jnp
from jax import lax
from jax.experimental import pallas as pl
from jax.experimental.pallas import tpu as pltpu
from jax.sharding import PartitionSpec as P

EPSILON = 1e-05
LOG2E = 1.4426950408889634
CHUNK = 128
LANES = 128
HALO = 16
BF = jnp.bfloat16
F32 = jnp.float32
VMEM_LIMIT = 60 * 1024 * 1024


def mm(a, b):
    return lax.dot_general(a, b, (((1,), (0,)), ((), ())), preferred_element_type=F32)


def nt(a, b):
    return lax.dot_general(a, b, (((1,), (1,)), ((), ())), preferred_element_type=F32)


def tn(a, b):
    return lax.dot_general(a, b, (((0,), (0,)), ((), ())), preferred_element_type=F32)


def lane_of(shape):
    return lax.broadcasted_iota(jnp.int32, shape, len(shape) - 1)


def row_of(shape):
    return lax.broadcasted_iota(jnp.int32, shape, len(shape) - 2)


def split_dup(v, rank):
    high = v.astype(BF)
    rest = (v - high.astype(F32)).astype(BF)
    return jnp.where(lane_of(v.shape) < rank, high, rest)


def fold(v, rank):
    return v[:rank] + v[rank : 2 * rank]


def expand(v, spread):
    high = v.astype(BF)
    rest = (v - high.astype(F32)).astype(BF)
    return mm(jnp.concatenate([high, rest], 1), spread)


def parts(v):
    high = v.astype(BF)
    return high, (v - high.astype(F32)).astype(BF)


def gather(v, emap):
    high, rest = parts(v)
    return nt(high, emap) + nt(rest, emap)


def both(product, a, b):
    if not isinstance(a, tuple):
        return product(a, b[0]) + product(a, b[1])
    if not isinstance(b, tuple):
        return product(a[0], b) + product(a[1], b)
    return product(a[0], b[0]) + product(a[0], b[1]) + product(a[1], b[0])


def paired(ws):
    return tuple(jnp.concatenate([ws[0][i], ws[1][i]], 1) for i in range(2))


def tri_sum(tri, v):
    a = v.astype(BF)
    r = v - a.astype(F32)
    b = r.astype(BF)
    c = (r - b.astype(F32)).astype(BF)
    w = v.shape[1]
    out = mm(tri, jnp.concatenate([a, b, c], 1))
    return out[:, :w] + out[:, w : 2 * w] + out[:, 2 * w :]


def sigm(v):
    return 0.5 * jnp.tanh(0.5 * v) + 0.5


def softplus(v):
    return jnp.maximum(v, 0.0) + jnp.log(1.0 + jnp.exp(-jnp.abs(v)))


def params(n):
    return pltpu.CompilerParams(
        dimension_semantics=("arbitrary",) * n, vmem_limit_bytes=VMEM_LIMIT
    )


def halves(v, h):
    w = v.shape[1] // 2
    lo, hi = v[:, :w], v[:, w:]
    return jnp.where(h == 0, lo, hi), jnp.where(h == 0, hi, lo)


def unweave_kernel(w, even, odd):
    n = w.shape[0]
    r = row_of((n, n))
    c = lane_of((n, n))
    m = (c == jnp.where(r < n // 2, 2 * r, 2 * r - n + 1)).astype(BF)
    out = mm(m, w[...]).astype(BF)
    even[...] = out[: n // 2]
    odd[...] = out[n // 2 :]


def front_kernel(
    tok, prev, halo, gain, wz, wx, wbc, wst, dn, upz, upx, cvx, cvb,
    z, xc, slx, bcc, slb, dtr, lrh, xs, bs, *, rank,
):
    t = pl.program_id(1)
    rows = tok.shape[1]

    def normed(v):
        f = v.astype(F32)
        scale = lax.rsqrt(jnp.mean(f * f, -1, keepdims=True) + EPSILON)
        return (f * scale * gain[...]).astype(BF)

    before = jnp.where(t == 0, halo[0], prev[0])
    ext = jnp.concatenate([normed(before), normed(tok[0])], 0)
    main = ext[HALO:]
    low = split_dup(nt(ext, dn[0]), rank)
    lrh[0] = low[HALO:]
    z[0] = (mm(main, wz[...]) + mm(low[HALO:], upz[0])).astype(BF)
    dtr[0] = mm(main, wst[...]).astype(BF).astype(F32)

    def conv(raw, keep, taps, act, slope):
        keep[...] = raw.astype(BF).astype(F32)
        pre = taps[4:5]
        for k in range(4):
            pre = pre + taps[k : k + 1] * keep[HALO - 3 + k : HALO - 3 + k + rows]
        s = sigm(pre)
        a = pre * s
        act[0] = a.astype(BF)
        slope[0] = s + a * (1.0 - s)

    conv(mm(ext, wx[...]) + mm(low, upx[0]), xs, cvx[...], xc, slx)
    conv(mm(ext, wbc[...]), bs, cvb[...], bcc, slb)


def state_kernel(dtr, xc, bcc, bias, na, spread, cum, vv, rc, cumT, vT, rs, sc, send, st, run):
    c = pl.program_id(1)
    q = CHUNK
    n = bcc.shape[2] // 2

    @pl.when(c == 0)
    def _():
        st[...] = jnp.zeros_like(st)
        run[...] = jnp.zeros_like(run)

    dt = softplus(dtr[0] + bias[...])
    tri = (row_of((q, q)) >= lane_of((q, q))).astype(BF)
    cm = tri_sum(tri, dt * na[...])
    v = cm - jnp.log2(dt)
    cum[0] = cm
    vv[0] = v
    rc[0] = cm + run[0:1]
    hr = cumT.shape[1]
    cumT[0] = jnp.transpose(cm)[:hr]
    vT[0] = jnp.transpose(v)[:hr]
    rs[0, 0] = run[...]
    sc[0, 0] = st[...]
    last = cm[q - 1 : q]
    w = expand(jnp.exp2(last - v), spread[...])
    wx = parts(w * xc[0].astype(F32))
    dec = expand(jnp.exp2(jnp.broadcast_to(last, (8, LANES))), spread[...])[0:1]
    st[...] = dec * st[...] + both(tn, bcc[0][:, :n], wx)
    run[...] = run[...] + last

    @pl.when(c == pl.num_programs(1) - 1)
    def _():
        send[0, :n] = st[...].astype(BF)
        total = expand(jnp.exp2(run[...]), spread[...])
        high = total.astype(BF)
        rest = (total - high.astype(F32)).astype(BF)
        send[0, n:] = jnp.concatenate([high, rest], 0)


def intra_kernel(xc, bcc, cum, vT, sc, skip, spread, y, *, heads):
    q = CHUNK
    n = bcc.shape[2] // 2
    b = bcc[0][:, :n]
    c = bcc[0][:, n:]
    scores = nt(c, b)
    allowed = row_of((q, q)) >= lane_of((q, q))
    cm = cum[0]
    e = expand(jnp.exp2(cm), spread[...])
    y[0] = both(mm, c, parts(sc[0, 0])) * e + skip[...] * xc[0].astype(F32)
    first = lane_of((q, LANES)) < LANES // 2
    for j in range(heads // 2):
        ws = []
        for h in (2 * j, 2 * j + 1):
            d = cm[:, h : h + 1] - vT[0, h : h + 1, :]
            ws.append(parts(jnp.exp2(jnp.where(allowed, d, -jnp.inf)) * scores))
        cols = slice(j * LANES, (j + 1) * LANES)
        xp = xc[0, :, cols]
        zero = jnp.zeros_like(xp)
        xbd = jnp.concatenate([jnp.where(first, xp, zero), jnp.where(first, zero, xp)], 0)
        y[0, :, cols] += both(mm, paired(ws), xbd)


def dnormout_kernel(g, wo, od, ou, dno, blh, *, rank):
    low = split_dup(nt(g[0], ou[0]), rank)
    blh[0] = low
    dno[0] = nt(g[0], wo[...]) + mm(low, od[0])


def gated_of(yl, bcc, rc, sin, z, spread):
    n = bcc.shape[2] // 2
    y = yl[0] + expand(jnp.exp2(rc[0]), spread[...]) * both(mm, bcc[0][:, n:], parts(sin[0]))
    gate = z[0].astype(F32)
    s = sigm(gate)
    return y, gate, s


def sums_kernel(yl, bcc, rc, sin, z, dno, og, spread, sums):
    y, gate, s = gated_of(yl, bcc, rc, sin, z, spread)
    gated = y * (gate * s)
    sq = jnp.sum(gated * gated, -1, keepdims=True)
    tot = jnp.sum(dno[0] * og[...] * gated, -1, keepdims=True)
    sums[0] = jnp.where(lane_of(sums.shape[1:]) == 0, sq, tot)


def gate_back_kernel(
    yl, bcc, rc, cum, sin, z, dno, sums, og, spread, no, dzr, dy, dc, send, dst, *, full
):
    step = pl.program_id(1)
    q = CHUNK
    n = bcc.shape[2] // 2

    @pl.when(step == 0)
    def _():
        dst[...] = jnp.zeros_like(dst)

    y, gate, s = gated_of(yl, bcc, rc, sin, z, spread)
    act = gate * s
    gated = y * act
    r = lax.rsqrt(sums[0][:, 0:1] / full + EPSILON)
    k = r * r * r * (sums[0][:, 1:2] / full)
    no[0] = (gated * r * og[...]).astype(BF)
    dg = r * (og[...] * dno[0]) - gated * k
    dzr[0] = (dg * y * (s + act * (1.0 - s))).astype(BF)
    dyv = dg * act
    dy[0] = dyv
    dc[0, 0] = dst[...]
    e = expand(jnp.exp2(cum[0]), spread[...])
    dst[...] = e[q - 1 : q] * dst[...] + both(tn, bcc[0][:, n:], parts(e * dyv))

    @pl.when(step == pl.num_programs(1) - 1)
    def _():
        send[0] = dst[...].astype(BF)


def out_kernel(head, no, g, tok, wo, od, ou, blh, keep, send, god, gou, *, rank):
    t = pl.program_id(1)

    @pl.when(t == 0)
    def _():
        god[...] = jnp.zeros_like(god)
        gou[...] = jnp.zeros_like(gou)

    low = split_dup(nt(no[0], od[0]), rank)
    own, other = halves(mm(no[0], wo[...]) + mm(low, ou[0]), head[0])
    keep[0] = own + halves(tok[0].astype(F32), head[0])[0]
    send[0] = other.astype(BF)
    god[0] += fold(tn(blh[0], no[0]), rank)
    gou[0] += fold(tn(low, g[0]), rank)


def scan_back_kernel(
    xc, bcc, dy, cumT, cum, vv, rc, rs, sc, sin, dc, dret, total, dtr, bias, na, skip, slx, slb,
    emap, spread, dpx, dpb, ddt, rowq, *, heads,
):
    q = CHUNK
    n = bcc.shape[2] // 2
    b = bcc[0][:, :n]
    c = bcc[0][:, n:]
    sT = nt(b, c)
    allowed = lane_of((q, q)) >= row_of((q, q))
    sT = jnp.where(allowed, sT, 0.0)
    cm = cum[0]
    v = vv[0]
    last = cm[q - 1 : q]
    first = lane_of((q, LANES)) < LANES // 2
    lanes = lane_of((q, LANES))
    rowq[...] = jnp.zeros_like(rowq)
    ds = jnp.zeros((q, q), F32)
    colq = jnp.zeros((q, LANES), F32)
    head8 = jnp.concatenate(
        [rs[0, 0][0:1], total[0][0:1] - rc[0][q - 1 : q], last, jnp.zeros((5, LANES), F32)], 0
    )
    decs = expand(jnp.exp2(head8), spread[...])
    s_in = sc[0, 0] + decs[0:1] * sin[0]
    d_out = dc[0, 0] + decs[1:2] * dret[0]
    s_two = parts(s_in)
    d_two = parts(d_out)
    x = xc[0].astype(F32)
    dyf = dy[0]
    e = expand(jnp.exp2(cm), spread[...])
    w = expand(jnp.exp2(last - v), spread[...])
    ed = e * dyf
    carried = both(mm, c, s_two)
    wbd = w * both(mm, b, d_two)
    wx = w * x
    up = gather(ed * carried, emap[...])
    vs = gather(x * wbd, emap[...])
    cross = gather(d_out * s_in, emap[...])
    crossed = jnp.sum(cross, 0, keepdims=True) * jnp.exp2(last)
    d_c = both(nt, parts(ed), s_two)
    d_b = both(nt, parts(wx), d_two)
    slope = slx[0]
    base = wbd + skip[...] * dyf
    for j in range(heads // 2):
        cols = slice(j * LANES, (j + 1) * LANES)
        xp = xc[0, :, cols]
        dbd = []
        for dp in parts(dyf[:, cols]):
            zero = jnp.zeros_like(dp)
            dbd.append(jnp.concatenate([jnp.where(first, dp, zero), jnp.where(first, zero, dp)], 0))
        dbd = tuple(dbd)
        dw = both(nt, xp, dbd)
        ws = []
        for i, h in enumerate((2 * j, 2 * j + 1)):
            d = cumT[0, h : h + 1, :] - v[:, h : h + 1]
            ex = jnp.exp2(jnp.where(allowed, d, -jnp.inf))
            ws.append(parts(ex * sT))
            dwe = dw[:, i * q : (i + 1) * q] * ex
            ds = ds + dwe
            qm = dwe * sT
            rowq[h : h + 1, :] = jnp.sum(qm, 0, keepdims=True)
            colq = jnp.where(lanes == h, jnp.sum(qm, 1, keepdims=True), colq)
        dx = both(mm, paired(ws), dbd) + base[:, cols]
        dpx[0, :, cols] = dx * slope[:, cols]
    ds_two = parts(ds)
    d_b = d_b + both(mm, ds_two, c)
    d_c = d_c + both(tn, ds_two, b)
    dpb[0] = jnp.concatenate([d_b, d_c], 1) * slb[0]
    rq = jnp.transpose(rowq[...])
    upper = (row_of((q, q)) <= lane_of((q, q))).astype(BF)
    lower = (row_of((q, q)) > lane_of((q, q))).astype(BF)
    dlog = tri_sum(upper, rq - colq + up) + tri_sum(lower, vs) + crossed
    raw = dtr[0] + bias[...]
    dt = softplus(raw)
    sg = jax.nn.sigmoid(raw)
    ratio = sg / jnp.maximum(dt, 1e-37)
    out = (colq + vs) * ratio + dlog * (na[...] * (1.0 / LOG2E)) * sg
    ddt[0] = jnp.where(lanes < heads, out, 0.0).astype(BF)


def back_kernel(
    head, dpx, nxx, hax, dpb, nxb, hab, dzr, ddt, tok, cot, gain, lrh, wz, wx, wbc, wst, dn, upz, upx, cvx, cvb,
    kept, send, giz, gix, gid, xs, bs, *, rank,
):
    t = pl.program_id(1)
    rows = tok.shape[1]
    end = t == pl.num_programs(1) - 1

    @pl.when(t == 0)
    def _():
        giz[...] = jnp.zeros_like(giz)
        gix[...] = jnp.zeros_like(gix)
        gid[...] = jnp.zeros_like(gid)

    def conv(tile, nxt, halo, keep, taps):
        keep[:rows] = tile[0]
        keep[rows:] = jnp.where(end, halo[0], nxt[0])
        out = taps[3:4] * keep[:rows]
        for k in range(3):
            out = out + taps[k : k + 1] * keep[3 - k : 3 - k + rows]
        return out.astype(BF)

    f = tok[0].astype(F32)
    scale = lax.rsqrt(jnp.mean(f * f, -1, keepdims=True) + EPSILON)
    nm = (f * scale * gain[...]).astype(BF)
    dz = dzr[0]
    dx = conv(dpx, nxx, hax, xs, cvx[...])
    db = conv(dpb, nxb, hab, bs, cvb[...])
    low = split_dup(nt(dz, upz[0]) + nt(dx, upx[0]), rank)
    out = nt(dz, wz[...]) + nt(dx, wx[...]) + nt(db, wbc[...]) + nt(ddt[0], wst[...])
    out = out + mm(low, dn[0])
    dg = out * gain[...]
    stat = jnp.sum(dg * f, -1, keepdims=True) / f.shape[1]
    own, other = halves(scale * dg - f * (scale * scale * scale * stat), head[0])
    kept[0] = own + halves(cot[0].astype(F32), head[0])[0]
    send[0] = other
    giz[0] += fold(tn(lrh[0], dz), rank)
    gix[0] += fold(tn(lrh[0], dx), rank)
    gid[0] += fold(tn(low, nm), rank)


def shift(x, axis, by):
    count = lax.axis_size(axis)
    return lax.ppermute(x, axis, [(i, i + by) for i in range(count) if 0 <= i + by < count])


def exchange_kernel(
    giz, gix, god, gid, gou, idx, out, pair, index, got, got2, s1, r1, s2, r2, s3, r3, s4, r4, s5, r5,
    s6, r6,
):
    nz, nb = lax.axis_size("seq"), lax.axis_size("batch")
    z, h, b = lax.axis_index("seq"), lax.axis_index("head"), lax.axis_index("batch")
    rows = giz.shape[0]
    w = giz.shape[1] // nz
    w2 = gid.shape[1] // (2 * nz)

    def plus(i, by, n):
        return lax.rem(i + by, n)

    def cut(p):
        return pl.ds(pl.multiple_of(p * w, w), w)

    def cut2(p, q):
        return pl.ds(pl.multiple_of((q * nz + p) * w2, w2), w2)

    def copy(src, dst, send, recv, **where):
        return pltpu.make_async_remote_copy(
            src_ref=src, dst_ref=dst, send_sem=send, recv_sem=recv, device_id=where,
            device_id_type=pl.DeviceIdType.MESH,
        )

    barrier = pltpu.get_barrier_semaphore()
    pairs = [(d, e) for d in range(nz) for e in range(2) if d or e]
    for d, e in pairs:
        pl.semaphore_signal(
            barrier, inc=1, device_id={"seq": plus(z, d, nz), "head": plus(h, e, 2)},
            device_id_type=pl.DeviceIdType.MESH,
        )
    for f in range(1, nb):
        pl.semaphore_signal(
            barrier, inc=1, device_id={"batch": plus(b, f, nb)},
            device_id_type=pl.DeviceIdType.MESH,
        )
    pl.semaphore_wait(barrier, len(pairs) + nb - 1)

    first = []
    for d in range(1, nz):
        p = plus(z, d, nz)
        for k, ref in enumerate((giz, gix, god)):
            first.append(copy(ref.at[:, cut(p)], got.at[k, d], s1.at[k, d], r1.at[k, d], seq=p))
    for i, (d, e) in enumerate(pairs):
        p, q = plus(z, d, nz), plus(h, e, 2)
        for k, ref in enumerate((gid, gou)):
            first.append(
                copy(ref.at[:, cut2(p, q)], got2.at[k, i], s2.at[k, i], r2.at[k, i], seq=p, head=q)
            )
    for f in range(1, nb):
        first.append(copy(idx, index.at[b], s3.at[f], r3.at[f], batch=plus(b, f, nb)))
    for c in first:
        c.start()
    index[b] = idx[...]
    for c in first:
        c.wait_recv()
    for k, ref in enumerate((giz, gix, god)):
        total = ref[:, cut(z)]
        for d in range(1, nz):
            total = total + got[k, d]
        out[b, z, k * rows : (k + 1) * rows] = total.astype(BF)
    parts = []
    for k, ref in enumerate((gid, gou)):
        total = ref[:, cut2(z, h)]
        for i in range(len(pairs)):
            total = total + got2[k, i]
        parts.append(total.astype(BF))
    out[b, z, 3 * rows :] = jnp.concatenate(parts, 1)
    for c in first:
        c.wait_send()

    sent = []

    def ship(k, src):
        for f in range(1, nb):
            c = copy(src, src, s5.at[k, f], r5.at[k, f], batch=plus(b, f, nb))
            c.start()
            sent.append(c)

    own = out.at[b, z]
    for d in range(1, nz):
        c = copy(own, own, s4.at[d], r4.at[d], seq=plus(z, d, nz))
        c.start()
        sent.append(c)
    ship(0, own)
    for d in range(1, nz):
        there = out.at[b, plus(z, nz - d, nz)]
        copy(there, there, s4.at[d], r4.at[d], seq=plus(z, d, nz)).wait_recv()
        ship(d, there)
    for d in range(nz):
        for f in range(1, nb):
            there = out.at[plus(b, nb - f, nb), plus(z, nz - d, nz)]
            copy(there, there, s5.at[d, f], r5.at[d, f], batch=plus(b, f, nb)).wait_recv()
    for c in sent:
        c.wait_send()
    last = copy(out.at[:, :, pl.ds(3 * rows, rows)], pair, s6, r6, head=plus(h, 1, 2))
    last.start()
    last.wait()


def table_kernel(idx, head, out, pair, up, od, idn, oup, *, seqs):
    nb, nz, _, w = out.shape
    rows = pair.shape[2]
    rank = od.shape[1]
    w2 = w // 2
    h = head[0]
    for ref in (up, od, idn, oup):
        ref[...] = jnp.zeros_like(ref)
    for b in range(nb):
        for s in range(seqs):
            a = idx[b * seqs + s]
            for z in range(nz):

                def part(ref, k):
                    return ref[b, z, k * rows + s * rank : k * rows + (s + 1) * rank].astype(F32)

                cols = slice(z * w, (z + 1) * w)
                up[a, 0, :, cols] += part(out, 0)
                up[a, 1, :, cols] += part(out, 1)
                od[a, :, cols] += part(out, 2)
                mine, other = part(out, 3), part(pair, 0)
                for q, v in ((0, jnp.where(h == 0, mine, other)), (1, jnp.where(h == 0, other, mine))):
                    cols = slice((q * nz + z) * w2, (q * nz + z + 1) * w2)
                    idn[a, :, cols] += v[:, :w2]
                    oup[a, :, cols] += v[:, w2:]


def exchange(giz, gix, god, gid, gou, adapter_index, head, adapters):
    S, R, I = giz.shape
    D = gid.shape[2]
    nz, nb = lax.axis_size("seq"), lax.axis_size("batch")
    rows = S * R
    w, w2 = I // nz, D // (2 * nz)
    if 2 * w2 != w:
        raise ValueError("widths differ")
    sds = jax.ShapeDtypeStruct
    dma = pltpu.SemaphoreType.DMA
    vmem = pl.BlockSpec(memory_space=pltpu.VMEM)
    smem = pl.BlockSpec(memory_space=pltpu.SMEM)
    flat = [v.reshape(rows, v.shape[2]) for v in (giz, gix, god, gid, gou)]
    idx = jnp.zeros((8, LANES), F32).at[0, :S].set(adapter_index.astype(F32))
    others = 2 * nz - 1
    out, pair, index = pl.pallas_call(
        exchange_kernel,
        in_specs=[vmem] * 6,
        out_specs=[vmem] * 3,
        out_shape=[sds((nb, nz, 4 * rows, w), BF), sds((nb, nz, rows, w), BF), sds((nb, 8, LANES), F32)],
        scratch_shapes=[
            pltpu.VMEM((3, nz, rows, w), F32), pltpu.VMEM((2, others, rows, w2), F32),
            dma((3, nz)), dma((3, nz)), dma((2, others)), dma((2, others)), dma((nb,)), dma((nb,)),
            dma((nz,)), dma((nz,)), dma((nz, nb)), dma((nz, nb)), dma, dma,
        ],
        compiler_params=pltpu.CompilerParams(collective_id=0, has_side_effects=True),
        name="exchange",
    )(*flat, idx)
    where = index[:, 0, :S].reshape(nb * S).astype(jnp.int32)
    up, od, idn, oup = pl.pallas_call(
        functools.partial(table_kernel, seqs=S),
        in_specs=[smem, smem, vmem, vmem],
        out_specs=[vmem] * 4,
        out_shape=[sds((adapters, 2, R, I), F32), sds((adapters, R, I), F32),
                   sds((adapters, R, D), F32), sds((adapters, R, D), F32)],
        compiler_params=pltpu.CompilerParams(vmem_limit_bytes=VMEM_LIMIT),
        name="tables",
    )(where, head, out, pair)
    return (jnp.swapaxes(idn, 1, 2), jnp.swapaxes(up, 1, 2), jnp.swapaxes(od, 1, 2), oup)


def local(
    tokens, cotangent, adapter_index, norm_gain, gate_input_weight, bc_weight, step_weight,
    conv_x, conv_bc, dt_bias, a_log, skip_gain, out_gain, output_weight,
    in_down, in_up, out_down, out_up,
):
    S, L, D = tokens.shape
    H = dt_bias.shape[0]
    I = output_weight.shape[0]
    N = bc_weight.shape[2] * lax.axis_size("head")
    NA = in_down.shape[0]
    R = in_down.shape[2]
    hp = I // H
    n_seq = lax.axis_size("seq")
    n_head = lax.axis_size("head")
    full = float(I * n_head)
    TB = min(256, L)
    half = D // n_head

    def swap(v):
        return lax.ppermute(v, "head", [(0, 1), (1, 0)])

    Q = CHUNK
    nc = L // Q
    HR = max(8, -(-H // 8) * 8)
    sds = jax.ShapeDtypeStruct

    UW = min(256, 2 * D)
    wz, wx = pl.pallas_call(
        unweave_kernel,
        grid=(2 * D // UW,),
        in_specs=[pl.BlockSpec((UW, I), lambda t: (t, 0))],
        out_specs=[pl.BlockSpec((UW // 2, I), lambda t: (t, 0))] * 2,
        out_shape=[sds((D, I), BF)] * 2,
        compiler_params=params(1),
        name="unweave",
    )(gate_input_weight.reshape(2 * D, I))
    head = lax.axis_index("head").astype(jnp.int32)[None]
    smem = pl.BlockSpec(memory_space=pltpu.SMEM)
    wbc = lax.all_gather(bc_weight, "head", axis=2, tiled=True).reshape(D, 2 * N)
    cvb = lax.all_gather(conv_bc, "head", axis=2, tiled=True).reshape(conv_bc.shape[0], 2 * N)
    wst = jnp.pad(step_weight, ((0, 0), (0, LANES - H)))
    onehot = (adapter_index[:, None] == jnp.arange(NA)[None, :]).astype(BF)

    def stack(rows):
        return jnp.concatenate(
            [rows, rows, jnp.zeros((S, LANES - 2 * R, rows.shape[2]), BF)], 1
        )

    def pick(spec, table):
        return jnp.einsum(spec, onehot, table, preferred_element_type=F32).astype(BF)

    dn = stack(pick("sa,adr->srd", in_down))
    up = pick("sa,arki->skri", in_up)
    upz = stack(up[:, 0])
    upx = stack(up[:, 1])
    od = stack(pick("sa,air->sri", out_down))
    ou = stack(pick("sa,ard->srd", out_up))
    emap = (jnp.arange(LANES)[:, None] == (jnp.arange(I) // hp)[None, :]).astype(BF)
    spread = jnp.concatenate([emap, emap], 0)

    def lanes(v):
        return jnp.pad(v, (0, LANES - H))[None]

    bias = lanes(dt_bias)
    na = lanes(-jnp.exp(a_log) * LOG2E)
    skip = jnp.repeat(skip_gain, hp)[None]
    gain = norm_gain[None]
    og = out_gain[None]

    def rows(width, tb, order=None):
        f = (lambda s, t: (s, t, 0)) if order is None else (lambda s, t: (s, order(t), 0))
        return pl.BlockSpec((1, tb, width), f)

    def whole(shape):
        return pl.BlockSpec(shape, lambda s, t: (0,) * len(shape))

    def per_seq(shape):
        return pl.BlockSpec((1,) + shape, lambda s, t: (s,) + (0,) * len(shape))

    def chunk4(a, b_, order=None):
        f = (lambda s, t: (s, t, 0, 0)) if order is None else (lambda s, t: (s, order(t), 0, 0))
        return pl.BlockSpec((1, 1, a, b_), f)

    halo = shift(tokens[:, L - HALO :], "seq", 1)
    per = TB // HALO
    grid = (S, L // TB)
    z, xc, slx, bcc, slb, dtr, lrh = pl.pallas_call(
        functools.partial(front_kernel, rank=R),
        grid=grid,
        in_specs=[
            rows(D, TB),
            pl.BlockSpec((1, HALO, D), lambda s, t: (s, jnp.maximum(t * per - 1, 0), 0)),
            per_seq((HALO, D)),
            whole((1, D)), whole((D, I)), whole((D, I)), whole((D, 2 * N)), whole((D, LANES)),
            per_seq((LANES, D)), per_seq((LANES, I)), per_seq((LANES, I)),
            whole(conv_x.shape), whole(cvb.shape),
        ],
        out_specs=[rows(I, TB), rows(I, TB), rows(I, TB), rows(2 * N, TB), rows(2 * N, TB),
                   rows(LANES, TB), rows(LANES, TB)],
        out_shape=[sds((S, L, I), BF), sds((S, L, I), BF), sds((S, L, I), F32),
                   sds((S, L, 2 * N), BF), sds((S, L, 2 * N), F32),
                   sds((S, L, LANES), F32), sds((S, L, LANES), BF)],
        scratch_shapes=[pltpu.VMEM((TB + HALO, I), F32), pltpu.VMEM((TB + HALO, 2 * N), F32)],
        compiler_params=params(2),
        name="front",
    )(tokens, tokens, halo, gain, wz, wx, wbc, wst, dn, upz, upx, conv_x, cvb)

    cgrid = (S, nc)
    tspec = pl.BlockSpec((1, HR, Q), lambda s, t: (s, 0, t))
    cum, vv, rc, cumT, vT, rs, sc, send = pl.pallas_call(
        state_kernel,
        grid=cgrid,
        in_specs=[rows(LANES, Q), rows(I, Q), rows(2 * N, Q), whole((1, LANES)), whole((1, LANES)),
                  whole((2 * LANES, I))],
        out_specs=[rows(LANES, Q), rows(LANES, Q), rows(LANES, Q), tspec, tspec,
                   chunk4(8, LANES), chunk4(N, I), per_seq((N + 16, I))],
        out_shape=[sds((S, L, LANES), F32)] * 3 + [sds((S, HR, L), F32)] * 2
        + [sds((S, nc, 8, LANES), F32), sds((S, nc, N, I), F32), sds((S, N + 16, I), BF)],
        scratch_shapes=[pltpu.VMEM((N, I), F32), pltpu.VMEM((8, LANES), F32)],
        compiler_params=params(2),
        name="states",
    )(dtr, xc, bcc, bias, na, spread)

    def gathered(v):
        return lax.all_gather(v, "seq")

    mine = lax.axis_index("seq")
    all_states = gathered(send)
    decays = (all_states[:, :, N : N + 1] .astype(F32) + all_states[:, :, N + 8 : N + 9].astype(F32))
    sin = jnp.zeros((S, N, I), F32)
    for p in range(n_seq - 1):
        sin = jnp.where(p < mine, sin * decays[p] + all_states[p, :, :N].astype(F32), sin)

    yl = pl.pallas_call(
        functools.partial(intra_kernel, heads=H),
        grid=cgrid,
        in_specs=[rows(I, Q), rows(2 * N, Q), rows(LANES, Q), tspec, chunk4(N, I), whole((1, I)),
                  whole((2 * LANES, I))],
        out_specs=rows(I, Q),
        out_shape=sds((S, L, I), F32),
        compiler_params=params(2),
        cost_estimate=pl.CostEstimate(
            flops=S * L * I * 8 * Q, bytes_accessed=S * L * I * 12, transcendentals=S * L * H * Q
        ),
        name="intra",
    )(xc, bcc, cum, vT, sc, skip, spread)

    dno, blh = pl.pallas_call(
        functools.partial(dnormout_kernel, rank=R),
        grid=grid,
        in_specs=[rows(D, TB), whole((I, D)), per_seq((LANES, I)), per_seq((LANES, D))],
        out_specs=[rows(I, TB), rows(LANES, TB)],
        out_shape=[sds((S, L, I), F32), sds((S, L, LANES), BF)],
        compiler_params=params(2),
        cost_estimate=pl.CostEstimate(
            flops=2 * S * L * I * D, bytes_accessed=S * L * (4 * I + 2 * D), transcendentals=0
        ),
        name="dnormout",
    )(cotangent, output_weight, od, ou)

    sums = pl.pallas_call(
        sums_kernel,
        grid=grid,
        in_specs=[rows(I, TB), rows(2 * N, TB), rows(LANES, TB), per_seq((N, I)), rows(I, TB),
                  rows(I, TB), whole((1, I)), whole((2 * LANES, I))],
        out_specs=rows(LANES, TB),
        out_shape=sds((S, L, LANES), F32),
        compiler_params=params(2),
        name="sums",
    )(yl, bcc, rc, sin, z, dno, og, spread)
    sums = lax.psum(sums[:, :, :2], "head")

    back = lambda t: nc - 1 - t
    no, dzr, dy, dc, dsend = pl.pallas_call(
        functools.partial(gate_back_kernel, full=full),
        grid=cgrid,
        in_specs=[rows(I, Q, back), rows(2 * N, Q, back), rows(LANES, Q, back), rows(LANES, Q, back),
                  per_seq((N, I)), rows(I, Q, back), rows(I, Q, back), rows(2, Q, back),
                  whole((1, I)), whole((2 * LANES, I))],
        out_specs=[rows(I, Q, back), rows(I, Q, back), rows(I, Q, back), chunk4(N, I, back),
                   per_seq((N, I))],
        out_shape=[sds((S, L, I), BF), sds((S, L, I), BF), sds((S, L, I), F32), sds((S, nc, N, I), F32), sds((S, N, I), BF)],
        scratch_shapes=[pltpu.VMEM((N, I), F32)],
        compiler_params=params(2),
        name="gate_back",
    )(yl, bcc, rc, cum, sin, z, dno, sums, og, spread)

    all_returned = gathered(dsend)
    dret = jnp.zeros((S, N, I), F32)
    for p in range(n_seq - 1, 0, -1):
        dret = jnp.where(p > mine, dret * decays[p] + all_returned[p].astype(F32), dret)

    keep, send_mix, god, gou = pl.pallas_call(
        functools.partial(out_kernel, rank=R),
        grid=grid,
        in_specs=[smem, rows(I, TB), rows(D, TB), rows(D, TB), whole((I, D)), per_seq((LANES, I)),
                  per_seq((LANES, D)), rows(LANES, TB)],
        out_specs=[rows(half, TB), rows(half, TB), per_seq((R, I)), per_seq((R, D))],
        out_shape=[sds((S, L, half), F32), sds((S, L, half), BF), sds((S, R, I), F32), sds((S, R, D), F32)],
        compiler_params=params(2),
        cost_estimate=pl.CostEstimate(
            flops=2 * S * L * I * D, bytes_accessed=S * L * (2 * I + 4 * D), transcendentals=0
        ),
        name="out_proj",
    )(head, no, cotangent, tokens, output_weight, od, ou, blh)
    result = (keep + swap(send_mix).astype(F32)).astype(BF)

    total = jnp.broadcast_to(rc[:, L - 1 : L], (S, 8, LANES))
    dpx, dpb, ddt = pl.pallas_call(
        functools.partial(scan_back_kernel, heads=H),
        grid=cgrid,
        in_specs=[rows(I, Q), rows(2 * N, Q), rows(I, Q), tspec, rows(LANES, Q), rows(LANES, Q),
                  rows(LANES, Q), chunk4(8, LANES), chunk4(N, I), per_seq((N, I)), chunk4(N, I),
                  per_seq((N, I)), per_seq((8, LANES)), rows(LANES, Q), whole((1, LANES)),
                  whole((1, LANES)), whole((1, I)), rows(I, Q), rows(2 * N, Q), whole((LANES, I)),
                  whole((2 * LANES, I))],
        out_specs=[rows(I, Q), rows(2 * N, Q), rows(LANES, Q)],
        out_shape=[sds((S, L, I), F32), sds((S, L, 2 * N), F32), sds((S, L, LANES), BF)],
        scratch_shapes=[pltpu.VMEM((LANES, Q), F32)],
        compiler_params=params(2),
        name="scan_back",
    )(xc, bcc, dy, cumT, cum, vv, rc, rs, sc, sin, dc, dret, total, dtr, bias, na, skip, slx, slb,
      emap, spread)

    hax = shift(dpx[:, :HALO], "seq", -1)
    hab = shift(dpb[:, :HALO], "seq", -1)
    last = L // HALO - 1
    after = lambda s, t: (s, jnp.minimum((t + 1) * per, last), 0)
    kept, send_grad, giz, gix, gid = pl.pallas_call(
        functools.partial(back_kernel, rank=R),
        grid=grid,
        in_specs=[
            smem, rows(I, TB), pl.BlockSpec((1, HALO, I), after), per_seq((HALO, I)),
            rows(2 * N, TB), pl.BlockSpec((1, HALO, 2 * N), after), per_seq((HALO, 2 * N)),
            rows(I, TB), rows(LANES, TB), rows(D, TB), rows(D, TB), whole((1, D)), rows(LANES, TB),
            whole((D, I)), whole((D, I)), whole((D, 2 * N)), whole((D, LANES)),
            per_seq((LANES, D)), per_seq((LANES, I)), per_seq((LANES, I)),
            whole(conv_x.shape), whole(cvb.shape),
        ],
        out_specs=[rows(half, TB), rows(half, TB), per_seq((R, I)), per_seq((R, I)),
                   per_seq((R, D))],
        out_shape=[sds((S, L, half), F32), sds((S, L, half), F32), sds((S, R, I), F32),
                   sds((S, R, I), F32), sds((S, R, D), F32)],
        scratch_shapes=[pltpu.VMEM((TB + HALO, I), F32), pltpu.VMEM((TB + HALO, 2 * N), F32)],
        compiler_params=params(2),
        name="in_back",
    )(head, dpx, dpx, hax, dpb, dpb, hab, dzr, ddt, tokens, cotangent, gain, lrh, wz, wx, wbc, wst, dn, upz, upx,
      conv_x, cvb)

    grad_tokens = (kept + swap(send_grad)).astype(BF)

    if n_head == 2 and I % (LANES * n_seq) == 0 and D % (2 * LANES * n_seq) == 0 and R % 16 == 0 and n_head * I == 2 * D:
        sums_of = exchange(giz, gix, god, gid, gou, adapter_index, head, NA)
        return (result, grad_tokens) + sums_of

    heads_part = jnp.stack([giz, gix, god], 1)
    shared_part = jnp.stack([gid, gou], 1)
    heads_part = lax.all_gather(lax.psum(heads_part, "seq"), "batch")
    shared_part = lax.all_gather(lax.psum(shared_part, ("seq", "head")), "batch")
    index = lax.all_gather(adapter_index, "batch")
    chosen = (index[:, :, None] == jnp.arange(NA)).astype(F32)

    def table(part):
        return jnp.einsum("bsa,bskri->akri", chosen, part, precision=lax.Precision.HIGHEST)

    heads_sum = table(heads_part)
    shared_sum = table(shared_part)
    grad_in_up = jnp.swapaxes(heads_sum[:, :2], 1, 2)
    grad_out_down = jnp.swapaxes(heads_sum[:, 2], 1, 2)
    grad_in_down = jnp.swapaxes(shared_sum[:, 0], 1, 2)
    grad_out_up = shared_sum[:, 1]
    return (result, grad_tokens, grad_in_down, grad_in_up, grad_out_down, grad_out_up)


def solution(mesh):
    in_specs = (
        P("batch", "seq", None),
        P("batch", "seq", None),
        P("batch"),
        P(),
        P(None, None, "head"),
        P(None, None, "head"),
        P(None, "head"),
        P(None, "head"),
        P(None, None, "head"),
        P("head"),
        P("head"),
        P("head"),
        P("head"),
        P("head", None),
        P(),
        P(None, None, None, "head"),
        P(None, "head", None),
        P(),
    )
    out_specs = (
        P("batch", "seq", "head"),
        P("batch", "seq", "head"),
        P(),
        P(None, None, None, "head"),
        P(None, "head", None),
        P(),
    )
    return jax.shard_map(local, mesh=mesh, in_specs=in_specs, out_specs=out_specs, check_vma=False)
```

```python
import functools

import jax
import jax.numpy as jnp
from jax import lax
from jax.experimental import pallas as pl
from jax.experimental.pallas import tpu as pltpu
from jax.sharding import PartitionSpec as P

EPSILON = 1e-05
LOG2E = 1.4426950408889634
CHUNK = 128
LANES = 128
HALO = 16
BF = jnp.bfloat16
F32 = jnp.float32
VMEM_LIMIT = 60 * 1024 * 1024


def mm(a, b):
    return lax.dot_general(a, b, (((1,), (0,)), ((), ())), preferred_element_type=F32)


def nt(a, b):
    return lax.dot_general(a, b, (((1,), (1,)), ((), ())), preferred_element_type=F32)


def tn(a, b):
    return lax.dot_general(a, b, (((0,), (0,)), ((), ())), preferred_element_type=F32)


def lane_of(shape):
    return lax.broadcasted_iota(jnp.int32, shape, len(shape) - 1)


def row_of(shape):
    return lax.broadcasted_iota(jnp.int32, shape, len(shape) - 2)


def split_dup(v, rank):
    high = v.astype(BF)
    rest = (v - high.astype(F32)).astype(BF)
    return jnp.where(lane_of(v.shape) < rank, high, rest)


def fold(v, rank):
    return v[:rank] + v[rank : 2 * rank]


def expand(v, spread):
    high = v.astype(BF)
    rest = (v - high.astype(F32)).astype(BF)
    return mm(jnp.concatenate([high, rest], 1), spread)


def parts(v):
    high = v.astype(BF)
    return high, (v - high.astype(F32)).astype(BF)


def gather(v, emap):
    high, rest = parts(v)
    return nt(high, emap) + nt(rest, emap)


def both(product, a, b):
    if not isinstance(a, tuple):
        return product(a, b[0]) + product(a, b[1])
    if not isinstance(b, tuple):
        return product(a[0], b) + product(a[1], b)
    return product(a[0], b[0]) + product(a[0], b[1]) + product(a[1], b[0])


def paired(ws):
    return tuple(jnp.concatenate([ws[0][i], ws[1][i]], 1) for i in range(2))


def tri_sum(tri, v):
    a = v.astype(BF)
    r = v - a.astype(F32)
    b = r.astype(BF)
    c = (r - b.astype(F32)).astype(BF)
    w = v.shape[1]
    out = mm(tri, jnp.concatenate([a, b, c], 1))
    return out[:, :w] + out[:, w : 2 * w] + out[:, 2 * w :]


def sigm(v):
    return 0.5 * jnp.tanh(0.5 * v) + 0.5


def softplus(v):
    return jnp.maximum(v, 0.0) + jnp.log(1.0 + jnp.exp(-jnp.abs(v)))


def params(n):
    return pltpu.CompilerParams(
        dimension_semantics=("arbitrary",) * n, vmem_limit_bytes=VMEM_LIMIT
    )


def halves(v, h):
    w = v.shape[1] // 2
    lo, hi = v[:, :w], v[:, w:]
    return jnp.where(h == 0, lo, hi), jnp.where(h == 0, hi, lo)


def unweave_kernel(w, even, odd):
    n = w.shape[0]
    r = row_of((n, n))
    c = lane_of((n, n))
    m = (c == jnp.where(r < n // 2, 2 * r, 2 * r - n + 1)).astype(BF)
    out = mm(m, w[...]).astype(BF)
    even[...] = out[: n // 2]
    odd[...] = out[n // 2 :]


def front_kernel(
    tok, prev, halo, gain, wz, wx, wbc, wst, dn, upz, upx, cvx, cvb,
    z, xc, slx, bcc, slb, dtr, lrh, xs, bs, *, rank,
):
    t = pl.program_id(1)
    rows = tok.shape[1]

    def normed(v):
        f = v.astype(F32)
        scale = lax.rsqrt(jnp.mean(f * f, -1, keepdims=True) + EPSILON)
        return (f * scale * gain[...]).astype(BF)

    before = jnp.where(t == 0, halo[0], prev[0])
    ext = jnp.concatenate([normed(before), normed(tok[0])], 0)
    main = ext[HALO:]
    low = split_dup(nt(ext, dn[0]), rank)
    lrh[0] = low[HALO:]
    z[0] = (mm(main, wz[...]) + mm(low[HALO:], upz[0])).astype(BF)
    dtr[0] = mm(main, wst[...]).astype(BF).astype(F32)

    def conv(raw, keep, taps, act, slope):
        keep[...] = raw.astype(BF).astype(F32)
        pre = taps[4:5]
        for k in range(4):
            pre = pre + taps[k : k + 1] * keep[HALO - 3 + k : HALO - 3 + k + rows]
        s = sigm(pre)
        a = pre * s
        act[0] = a.astype(BF)
        slope[0] = s + a * (1.0 - s)

    conv(mm(ext, wx[...]) + mm(low, upx[0]), xs, cvx[...], xc, slx)
    conv(mm(ext, wbc[...]), bs, cvb[...], bcc, slb)


def state_kernel(dtr, xc, bcc, bias, na, spread, cum, vv, rc, cumT, vT, rs, sc, send, st, run):
    c = pl.program_id(1)
    q = CHUNK
    n = bcc.shape[2] // 2

    @pl.when(c == 0)
    def _():
        st[...] = jnp.zeros_like(st)
        run[...] = jnp.zeros_like(run)

    dt = softplus(dtr[0] + bias[...])
    tri = (row_of((q, q)) >= lane_of((q, q))).astype(BF)
    cm = tri_sum(tri, dt * na[...])
    v = cm - jnp.log2(dt)
    cum[0] = cm
    vv[0] = v
    rc[0] = cm + run[0:1]
    hr = cumT.shape[1]
    cumT[0] = jnp.transpose(cm)[:hr]
    vT[0] = jnp.transpose(v)[:hr]
    rs[0, 0] = run[...]
    sc[0, 0] = st[...]
    last = cm[q - 1 : q]
    w = expand(jnp.exp2(last - v), spread[...])
    wx = parts(w * xc[0].astype(F32))
    dec = expand(jnp.exp2(jnp.broadcast_to(last, (8, LANES))), spread[...])[0:1]
    st[...] = dec * st[...] + both(tn, bcc[0][:, :n], wx)
    run[...] = run[...] + last

    @pl.when(c == pl.num_programs(1) - 1)
    def _():
        send[0, :n] = st[...].astype(BF)
        total = expand(jnp.exp2(run[...]), spread[...])
        high = total.astype(BF)
        rest = (total - high.astype(F32)).astype(BF)
        send[0, n:] = jnp.concatenate([high, rest], 0)


def intra_kernel(xc, bcc, cum, vT, sc, skip, spread, y, *, heads):
    q = CHUNK
    n = bcc.shape[2] // 2
    b = bcc[0][:, :n]
    c = bcc[0][:, n:]
    scores = nt(c, b)
    allowed = row_of((q, q)) >= lane_of((q, q))
    cm = cum[0]
    e = expand(jnp.exp2(cm), spread[...])
    y[0] = both(mm, c, parts(sc[0, 0])) * e + skip[...] * xc[0].astype(F32)
    first = lane_of((q, LANES)) < LANES // 2
    for j in range(heads // 2):
        ws = []
        for h in (2 * j, 2 * j + 1):
            d = cm[:, h : h + 1] - vT[0, h : h + 1, :]
            ws.append(parts(jnp.exp2(jnp.where(allowed, d, -jnp.inf)) * scores))
        cols = slice(j * LANES, (j + 1) * LANES)
        xp = xc[0, :, cols]
        zero = jnp.zeros_like(xp)
        xbd = jnp.concatenate([jnp.where(first, xp, zero), jnp.where(first, zero, xp)], 0)
        y[0, :, cols] += both(mm, paired(ws), xbd)


def dnormout_kernel(g, wo, od, ou, dno, blh, *, rank):
    low = split_dup(nt(g[0], ou[0]), rank)
    blh[0] = low
    dno[0] = nt(g[0], wo[...]) + mm(low, od[0])


def gated_of(yl, bcc, rc, sin, z, spread):
    n = bcc.shape[2] // 2
    y = yl[0] + expand(jnp.exp2(rc[0]), spread[...]) * both(mm, bcc[0][:, n:], parts(sin[0]))
    gate = z[0].astype(F32)
    s = sigm(gate)
    return y, gate, s


def sums_kernel(yl, bcc, rc, sin, z, dno, og, spread, sums):
    y, gate, s = gated_of(yl, bcc, rc, sin, z, spread)
    gated = y * (gate * s)
    sq = jnp.sum(gated * gated, -1, keepdims=True)
    tot = jnp.sum(dno[0] * og[...] * gated, -1, keepdims=True)
    both_sums = jnp.where(lane_of((sq.shape[0], LANES)) == 0, sq, tot)
    sums[0] = jnp.transpose(both_sums)[:8]


def gate_back_kernel(
    yl, bcc, rc, cum, sin, z, dno, mine, other, og, spread, no, dzr, dy, dc, send, dst, *, full
):
    step = pl.program_id(1)
    q = CHUNK
    n = bcc.shape[2] // 2

    @pl.when(step == 0)
    def _():
        dst[...] = jnp.zeros_like(dst)

    y, gate, s = gated_of(yl, bcc, rc, sin, z, spread)
    act = gate * s
    gated = y * act
    sums = mine[0] + other[0]
    sums = jnp.transpose(jnp.concatenate([sums, jnp.zeros((LANES - 8, q), F32)], 0))
    r = lax.rsqrt(sums[:, 0:1] / full + EPSILON)
    k = r * r * r * (sums[:, 1:2] / full)
    no[0] = (gated * r * og[...]).astype(BF)
    dg = r * (og[...] * dno[0]) - gated * k
    dzr[0] = (dg * y * (s + act * (1.0 - s))).astype(BF)
    dyv = dg * act
    dy[0] = dyv
    dc[0, 0] = dst[...]
    e = expand(jnp.exp2(cum[0]), spread[...])
    dst[...] = e[q - 1 : q] * dst[...] + both(tn, bcc[0][:, n:], parts(e * dyv))

    @pl.when(step == pl.num_programs(1) - 1)
    def _():
        send[0] = dst[...].astype(BF)


def out_kernel(head, no, g, tok, wo, od, ou, blh, keep, send, god, gou, *, rank):
    t = pl.program_id(1)

    @pl.when(t == 0)
    def _():
        god[...] = jnp.zeros_like(god)
        gou[...] = jnp.zeros_like(gou)

    low = split_dup(nt(no[0], od[0]), rank)
    own, other = halves(mm(no[0], wo[...]) + mm(low, ou[0]), head[0])
    keep[0] = own + halves(tok[0].astype(F32), head[0])[0]
    send[0] = other.astype(BF)
    god[0] += fold(tn(blh[0], no[0]), rank)
    gou[0] += fold(tn(low, g[0]), rank)


def scan_back_kernel(
    xc, bcc, dy, cumT, cum, vv, rc, rs, sc, sin, dc, dret, total, dtr, bias, na, skip, slx, slb,
    emap, spread, dpx, dpb, ddt, rowq, *, heads,
):
    q = CHUNK
    n = bcc.shape[2] // 2
    b = bcc[0][:, :n]
    c = bcc[0][:, n:]
    sT = nt(b, c)
    allowed = lane_of((q, q)) >= row_of((q, q))
    sT = jnp.where(allowed, sT, 0.0)
    cm = cum[0]
    v = vv[0]
    last = cm[q - 1 : q]
    first = lane_of((q, LANES)) < LANES // 2
    lanes = lane_of((q, LANES))
    rowq[...] = jnp.zeros_like(rowq)
    ds = jnp.zeros((q, q), F32)
    colq = jnp.zeros((q, LANES), F32)
    head8 = jnp.concatenate(
        [rs[0, 0][0:1], total[0][0:1] - rc[0][q - 1 : q], last, jnp.zeros((5, LANES), F32)], 0
    )
    decs = expand(jnp.exp2(head8), spread[...])
    s_in = sc[0, 0] + decs[0:1] * sin[0]
    d_out = dc[0, 0] + decs[1:2] * dret[0]
    s_two = parts(s_in)
    d_two = parts(d_out)
    x = xc[0].astype(F32)
    dyf = dy[0]
    e = expand(jnp.exp2(cm), spread[...])
    w = expand(jnp.exp2(last - v), spread[...])
    ed = e * dyf
    carried = both(mm, c, s_two)
    wbd = w * both(mm, b, d_two)
    wx = w * x
    up = gather(ed * carried, emap[...])
    vs = gather(x * wbd, emap[...])
    cross = gather(d_out * s_in, emap[...])
    crossed = jnp.sum(cross, 0, keepdims=True) * jnp.exp2(last)
    d_c = both(nt, parts(ed), s_two)
    d_b = both(nt, parts(wx), d_two)
    slope = slx[0]
    base = wbd + skip[...] * dyf
    for j in range(heads // 2):
        cols = slice(j * LANES, (j + 1) * LANES)
        xp = xc[0, :, cols]
        dbd = []
        for dp in parts(dyf[:, cols]):
            zero = jnp.zeros_like(dp)
            dbd.append(jnp.concatenate([jnp.where(first, dp, zero), jnp.where(first, zero, dp)], 0))
        dbd = tuple(dbd)
        dw = both(nt, xp, dbd)
        ws = []
        for i, h in enumerate((2 * j, 2 * j + 1)):
            d = cumT[0, h : h + 1, :] - v[:, h : h + 1]
            ex = jnp.exp2(jnp.where(allowed, d, -jnp.inf))
            ws.append(parts(ex * sT))
            dwe = dw[:, i * q : (i + 1) * q] * ex
            ds = ds + dwe
            qm = dwe * sT
            rowq[h : h + 1, :] = jnp.sum(qm, 0, keepdims=True)
            colq = jnp.where(lanes == h, jnp.sum(qm, 1, keepdims=True), colq)
        dx = both(mm, paired(ws), dbd) + base[:, cols]
        dpx[0, :, cols] = dx * slope[:, cols]
    ds_two = parts(ds)
    d_b = d_b + both(mm, ds_two, c)
    d_c = d_c + both(tn, ds_two, b)
    dpb[0] = jnp.concatenate([d_b, d_c], 1) * slb[0]
    rq = jnp.transpose(rowq[...])
    upper = (row_of((q, q)) <= lane_of((q, q))).astype(BF)
    lower = (row_of((q, q)) > lane_of((q, q))).astype(BF)
    dlog = tri_sum(upper, rq - colq + up) + tri_sum(lower, vs) + crossed
    raw = dtr[0] + bias[...]
    dt = softplus(raw)
    sg = jax.nn.sigmoid(raw)
    ratio = sg / jnp.maximum(dt, 1e-37)
    out = (colq + vs) * ratio + dlog * (na[...] * (1.0 / LOG2E)) * sg
    ddt[0] = jnp.where(lanes < heads, out, 0.0).astype(BF)


def back_kernel(
    head, dpx, nxx, hax, dpb, nxb, hab, dzr, ddt, tok, cot, gain, lrh, wz, wx, wbc, wst, dn, upz, upx, cvx, cvb,
    kept, send, giz, gix, gid, xs, bs, *, rank,
):
    t = pl.program_id(1)
    rows = tok.shape[1]
    end = t == pl.num_programs(1) - 1

    @pl.when(t == 0)
    def _():
        giz[...] = jnp.zeros_like(giz)
        gix[...] = jnp.zeros_like(gix)
        gid[...] = jnp.zeros_like(gid)

    def conv(tile, nxt, halo, keep, taps):
        keep[:rows] = tile[0]
        keep[rows:] = jnp.where(end, halo[0], nxt[0])
        out = taps[3:4] * keep[:rows]
        for k in range(3):
            out = out + taps[k : k + 1] * keep[3 - k : 3 - k + rows]
        return out.astype(BF)

    f = tok[0].astype(F32)
    scale = lax.rsqrt(jnp.mean(f * f, -1, keepdims=True) + EPSILON)
    nm = (f * scale * gain[...]).astype(BF)
    dz = dzr[0]
    dx = conv(dpx, nxx, hax, xs, cvx[...])
    db = conv(dpb, nxb, hab, bs, cvb[...])
    low = split_dup(nt(dz, upz[0]) + nt(dx, upx[0]), rank)
    out = nt(dz, wz[...]) + nt(dx, wx[...]) + nt(db, wbc[...]) + nt(ddt[0], wst[...])
    out = out + mm(low, dn[0])
    dg = out * gain[...]
    stat = jnp.sum(dg * f, -1, keepdims=True) / f.shape[1]
    own, other = halves(scale * dg - f * (scale * scale * scale * stat), head[0])
    kept[0] = own + halves(cot[0].astype(F32), head[0])[0]
    send[0] = other
    giz[0] += fold(tn(lrh[0], dz), rank)
    gix[0] += fold(tn(lrh[0], dx), rank)
    gid[0] += fold(tn(low, nm), rank)


def shift(x, axis, by):
    count = lax.axis_size(axis)
    return lax.ppermute(x, axis, [(i, i + by) for i in range(count) if 0 <= i + by < count])


def exchange_kernel(
    giz, gix, god, gid, gou, idx, out, pair, index, got, got2, s1, r1, s2, r2, s3, r3, s4, r4, s5, r5,
    s6, r6,
):
    nz, nb = lax.axis_size("seq"), lax.axis_size("batch")
    z, h, b = lax.axis_index("seq"), lax.axis_index("head"), lax.axis_index("batch")
    rows = giz.shape[0]
    w = giz.shape[1] // nz
    w2 = gid.shape[1] // (2 * nz)

    def plus(i, by, n):
        return lax.rem(i + by, n)

    def cut(p):
        return pl.ds(pl.multiple_of(p * w, w), w)

    def cut2(p, q):
        return pl.ds(pl.multiple_of((q * nz + p) * w2, w2), w2)

    def copy(src, dst, send, recv, **where):
        return pltpu.make_async_remote_copy(
            src_ref=src, dst_ref=dst, send_sem=send, recv_sem=recv, device_id=where,
            device_id_type=pl.DeviceIdType.MESH,
        )

    barrier = pltpu.get_barrier_semaphore()
    pairs = [(d, e) for d in range(nz) for e in range(2) if d or e]
    for d, e in pairs:
        pl.semaphore_signal(
            barrier, inc=1, device_id={"seq": plus(z, d, nz), "head": plus(h, e, 2)},
            device_id_type=pl.DeviceIdType.MESH,
        )
    for f in range(1, nb):
        pl.semaphore_signal(
            barrier, inc=1, device_id={"batch": plus(b, f, nb)},
            device_id_type=pl.DeviceIdType.MESH,
        )
    pl.semaphore_wait(barrier, len(pairs) + nb - 1)

    first = []
    for d in range(1, nz):
        p = plus(z, d, nz)
        for k, ref in enumerate((giz, gix, god)):
            first.append(copy(ref.at[:, cut(p)], got.at[k, d], s1.at[k, d], r1.at[k, d], seq=p))
    for i, (d, e) in enumerate(pairs):
        p, q = plus(z, d, nz), plus(h, e, 2)
        for k, ref in enumerate((gid, gou)):
            first.append(
                copy(ref.at[:, cut2(p, q)], got2.at[k, i], s2.at[k, i], r2.at[k, i], seq=p, head=q)
            )
    for f in range(1, nb):
        first.append(copy(idx, index.at[b], s3.at[f], r3.at[f], batch=plus(b, f, nb)))
    for c in first:
        c.start()
    index[b] = idx[...]
    for c in first:
        c.wait_recv()
    for k, ref in enumerate((giz, gix, god)):
        total = ref[:, cut(z)]
        for d in range(1, nz):
            total = total + got[k, d]
        out[b, z, k * rows : (k + 1) * rows] = total.astype(BF)
    parts = []
    for k, ref in enumerate((gid, gou)):
        total = ref[:, cut2(z, h)]
        for i in range(len(pairs)):
            total = total + got2[k, i]
        parts.append(total.astype(BF))
    out[b, z, 3 * rows :] = jnp.concatenate(parts, 1)
    for c in first:
        c.wait_send()

    sent = []

    def ship(k, src):
        for f in range(1, nb):
            c = copy(src, src, s5.at[k, f], r5.at[k, f], batch=plus(b, f, nb))
            c.start()
            sent.append(c)

    own = out.at[b, z]
    for d in range(1, nz):
        c = copy(own, own, s4.at[d], r4.at[d], seq=plus(z, d, nz))
        c.start()
        sent.append(c)
    ship(0, own)
    for d in range(1, nz):
        there = out.at[b, plus(z, nz - d, nz)]
        copy(there, there, s4.at[d], r4.at[d], seq=plus(z, d, nz)).wait_recv()
        ship(d, there)
    for d in range(nz):
        for f in range(1, nb):
            there = out.at[plus(b, nb - f, nb), plus(z, nz - d, nz)]
            copy(there, there, s5.at[d, f], r5.at[d, f], batch=plus(b, f, nb)).wait_recv()
    for c in sent:
        c.wait_send()
    last = copy(out.at[:, :, pl.ds(3 * rows, rows)], pair, s6, r6, head=plus(h, 1, 2))
    last.start()
    last.wait()


def table_kernel(idx, head, out, pair, up, od, idn, oup, *, seqs):
    nb, nz, _, w = out.shape
    rows = pair.shape[2]
    rank = od.shape[1]
    w2 = w // 2
    h = head[0]
    for ref in (up, od, idn, oup):
        ref[...] = jnp.zeros_like(ref)
    for b in range(nb):
        for s in range(seqs):
            a = idx[b * seqs + s]
            for z in range(nz):

                def part(ref, k):
                    return ref[b, z, k * rows + s * rank : k * rows + (s + 1) * rank].astype(F32)

                cols = slice(z * w, (z + 1) * w)
                up[a, 0, :, cols] += part(out, 0)
                up[a, 1, :, cols] += part(out, 1)
                od[a, :, cols] += part(out, 2)
                mine, other = part(out, 3), part(pair, 0)
                for q, v in ((0, jnp.where(h == 0, mine, other)), (1, jnp.where(h == 0, other, mine))):
                    cols = slice((q * nz + z) * w2, (q * nz + z + 1) * w2)
                    idn[a, :, cols] += v[:, :w2]
                    oup[a, :, cols] += v[:, w2:]


def exchange(giz, gix, god, gid, gou, adapter_index, head, adapters):
    S, R, I = giz.shape
    D = gid.shape[2]
    nz, nb = lax.axis_size("seq"), lax.axis_size("batch")
    rows = S * R
    w, w2 = I // nz, D // (2 * nz)
    if 2 * w2 != w:
        raise ValueError("widths differ")
    sds = jax.ShapeDtypeStruct
    dma = pltpu.SemaphoreType.DMA
    vmem = pl.BlockSpec(memory_space=pltpu.VMEM)
    smem = pl.BlockSpec(memory_space=pltpu.SMEM)
    flat = [v.reshape(rows, v.shape[2]) for v in (giz, gix, god, gid, gou)]
    idx = jnp.zeros((8, LANES), F32).at[0, :S].set(adapter_index.astype(F32))
    others = 2 * nz - 1
    out, pair, index = pl.pallas_call(
        exchange_kernel,
        in_specs=[vmem] * 6,
        out_specs=[vmem] * 3,
        out_shape=[sds((nb, nz, 4 * rows, w), BF), sds((nb, nz, rows, w), BF), sds((nb, 8, LANES), F32)],
        scratch_shapes=[
            pltpu.VMEM((3, nz, rows, w), F32), pltpu.VMEM((2, others, rows, w2), F32),
            dma((3, nz)), dma((3, nz)), dma((2, others)), dma((2, others)), dma((nb,)), dma((nb,)),
            dma((nz,)), dma((nz,)), dma((nz, nb)), dma((nz, nb)), dma, dma,
        ],
        compiler_params=pltpu.CompilerParams(collective_id=0, has_side_effects=True),
        name="exchange",
    )(*flat, idx)
    where = index[:, 0, :S].reshape(nb * S).astype(jnp.int32)
    up, od, idn, oup = pl.pallas_call(
        functools.partial(table_kernel, seqs=S),
        in_specs=[smem, smem, vmem, vmem],
        out_specs=[vmem] * 4,
        out_shape=[sds((adapters, 2, R, I), F32), sds((adapters, R, I), F32),
                   sds((adapters, R, D), F32), sds((adapters, R, D), F32)],
        compiler_params=pltpu.CompilerParams(vmem_limit_bytes=VMEM_LIMIT),
        name="tables",
    )(where, head, out, pair)
    return (jnp.swapaxes(idn, 1, 2), jnp.swapaxes(up, 1, 2), jnp.swapaxes(od, 1, 2), oup)


def local(
    tokens, cotangent, adapter_index, norm_gain, gate_input_weight, bc_weight, step_weight,
    conv_x, conv_bc, dt_bias, a_log, skip_gain, out_gain, output_weight,
    in_down, in_up, out_down, out_up,
):
    S, L, D = tokens.shape
    H = dt_bias.shape[0]
    I = output_weight.shape[0]
    N = bc_weight.shape[2] * lax.axis_size("head")
    NA = in_down.shape[0]
    R = in_down.shape[2]
    hp = I // H
    n_seq = lax.axis_size("seq")
    n_head = lax.axis_size("head")
    full = float(I * n_head)
    TB = min(256, L)
    half = D // n_head

    def swap(v):
        return lax.ppermute(v, "head", [(0, 1), (1, 0)])

    Q = CHUNK
    nc = L // Q
    HR = max(8, -(-H // 8) * 8)
    sds = jax.ShapeDtypeStruct

    UW = min(256, 2 * D)
    wz, wx = pl.pallas_call(
        unweave_kernel,
        grid=(2 * D // UW,),
        in_specs=[pl.BlockSpec((UW, I), lambda t: (t, 0))],
        out_specs=[pl.BlockSpec((UW // 2, I), lambda t: (t, 0))] * 2,
        out_shape=[sds((D, I), BF)] * 2,
        compiler_params=params(1),
        name="unweave",
    )(gate_input_weight.reshape(2 * D, I))
    head = lax.axis_index("head").astype(jnp.int32)[None]
    smem = pl.BlockSpec(memory_space=pltpu.SMEM)
    wbc = lax.all_gather(bc_weight, "head", axis=2, tiled=True).reshape(D, 2 * N)
    cvb = lax.all_gather(conv_bc, "head", axis=2, tiled=True).reshape(conv_bc.shape[0], 2 * N)
    wst = jnp.pad(step_weight, ((0, 0), (0, LANES - H)))
    onehot = (adapter_index[:, None] == jnp.arange(NA)[None, :]).astype(BF)

    def stack(rows):
        return jnp.concatenate(
            [rows, rows, jnp.zeros((S, LANES - 2 * R, rows.shape[2]), BF)], 1
        )

    def pick(spec, table):
        return jnp.einsum(spec, onehot, table, preferred_element_type=F32).astype(BF)

    dn = stack(pick("sa,adr->srd", in_down))
    up = pick("sa,arki->skri", in_up)
    upz = stack(up[:, 0])
    upx = stack(up[:, 1])
    od = stack(pick("sa,air->sri", out_down))
    ou = stack(pick("sa,ard->srd", out_up))
    emap = (jnp.arange(LANES)[:, None] == (jnp.arange(I) // hp)[None, :]).astype(BF)
    spread = jnp.concatenate([emap, emap], 0)

    def lanes(v):
        return jnp.pad(v, (0, LANES - H))[None]

    bias = lanes(dt_bias)
    na = lanes(-jnp.exp(a_log) * LOG2E)
    skip = jnp.repeat(skip_gain, hp)[None]
    gain = norm_gain[None]
    og = out_gain[None]

    def rows(width, tb, order=None):
        f = (lambda s, t: (s, t, 0)) if order is None else (lambda s, t: (s, order(t), 0))
        return pl.BlockSpec((1, tb, width), f)

    def whole(shape):
        return pl.BlockSpec(shape, lambda s, t: (0,) * len(shape))

    def per_seq(shape):
        return pl.BlockSpec((1,) + shape, lambda s, t: (s,) + (0,) * len(shape))

    def chunk4(a, b_, order=None):
        f = (lambda s, t: (s, t, 0, 0)) if order is None else (lambda s, t: (s, order(t), 0, 0))
        return pl.BlockSpec((1, 1, a, b_), f)

    def staged(kernel, name, one, in_specs, args, outs, prev, scratch=()):
        def at(spec):
            if spec.index_map is None:
                return spec
            return pl.BlockSpec(spec.block_shape, lambda s, t: spec.index_map(one, t))

        shared = [i for i, o in enumerate(outs) if o[2]] if prev else []
        n = len(args)

        def body(*refs):
            kernel(*refs[:n], *refs[n + len(shared) :])

        return pl.pallas_call(
            body,
            grid=(1, nc),
            in_specs=[at(v) for v in in_specs] + [pl.BlockSpec(memory_space=pl.ANY)] * len(shared),
            out_specs=[at(o[0]) for o in outs],
            out_shape=[o[1] for o in outs],
            scratch_shapes=list(scratch),
            input_output_aliases={n + i: k for i, k in enumerate(shared)},
            compiler_params=params(2),
            name=name,
        )(*args, *[prev[k] for k in shared])

    halo = shift(tokens[:, L - HALO :], "seq", 1)
    per = TB // HALO
    grid = (S, L // TB)
    z, xc, slx, bcc, slb, dtr, lrh = pl.pallas_call(
        functools.partial(front_kernel, rank=R),
        grid=grid,
        in_specs=[
            rows(D, TB),
            pl.BlockSpec((1, HALO, D), lambda s, t: (s, jnp.maximum(t * per - 1, 0), 0)),
            per_seq((HALO, D)),
            whole((1, D)), whole((D, I)), whole((D, I)), whole((D, 2 * N)), whole((D, LANES)),
            per_seq((LANES, D)), per_seq((LANES, I)), per_seq((LANES, I)),
            whole(conv_x.shape), whole(cvb.shape),
        ],
        out_specs=[rows(I, TB), rows(I, TB), rows(I, TB), rows(2 * N, TB), rows(2 * N, TB),
                   rows(LANES, TB), rows(LANES, TB)],
        out_shape=[sds((S, L, I), BF), sds((S, L, I), BF), sds((S, L, I), F32),
                   sds((S, L, 2 * N), BF), sds((S, L, 2 * N), F32),
                   sds((S, L, LANES), F32), sds((S, L, LANES), BF)],
        scratch_shapes=[pltpu.VMEM((TB + HALO, I), F32), pltpu.VMEM((TB + HALO, 2 * N), F32)],
        compiler_params=params(2),
        name="front",
    )(tokens, tokens, halo, gain, wz, wx, wbc, wst, dn, upz, upx, conv_x, cvb)

    cgrid = (S, nc)
    tspec = pl.BlockSpec((1, HR, Q), lambda s, t: (s, 0, t))
    lane_rows = (rows(LANES, Q), sds((S, L, LANES), F32), True)
    head_rows = (tspec, sds((S, HR, L), F32), True)
    state_outs = [
        lane_rows, lane_rows, lane_rows, head_rows, head_rows,
        (chunk4(8, LANES), sds((S, nc, 8, LANES), F32), True),
        (chunk4(N, I), sds((S, nc, N, I), F32), True),
        (whole((1, N + 16, I)), sds((1, N + 16, I), BF), False),
    ]
    mine = lax.axis_index("seq")
    states, sends = None, []
    for one in range(S):
        states = staged(
            state_kernel, "states", one,
            [rows(LANES, Q), rows(I, Q), rows(2 * N, Q), whole((1, LANES)), whole((1, LANES)),
             whole((2 * LANES, I))],
            (dtr, xc, bcc, bias, na, spread), state_outs, states,
            (pltpu.VMEM((N, I), F32), pltpu.VMEM((8, LANES), F32)),
        )
        sends.append(states[-1])
    cum, vv, rc, cumT, vT, rs, sc = states[:7]
    sins, decays = [], []
    for send in sends:
        all_states = lax.all_gather(send, "seq")
        dec = all_states[:, :, N : N + 1].astype(F32) + all_states[:, :, N + 8 : N + 9].astype(F32)
        sin = jnp.zeros((1, N, I), F32)
        for p in range(n_seq - 1):
            sin = jnp.where(p < mine, sin * dec[p] + all_states[p, :, :N].astype(F32), sin)
        sins.append(sin)
        decays.append(dec)

    yl = pl.pallas_call(
        functools.partial(intra_kernel, heads=H),
        grid=cgrid,
        in_specs=[rows(I, Q), rows(2 * N, Q), rows(LANES, Q), tspec, chunk4(N, I), whole((1, I)),
                  whole((2 * LANES, I))],
        out_specs=rows(I, Q),
        out_shape=sds((S, L, I), F32),
        compiler_params=params(2),
        cost_estimate=pl.CostEstimate(
            flops=S * L * I * 8 * Q, bytes_accessed=S * L * I * 12, transcendentals=S * L * H * Q
        ),
        name="intra",
    )(xc, bcc, cum, vT, sc, skip, spread)

    dno, blh = pl.pallas_call(
        functools.partial(dnormout_kernel, rank=R),
        grid=grid,
        in_specs=[rows(D, TB), whole((I, D)), per_seq((LANES, I)), per_seq((LANES, D))],
        out_specs=[rows(I, TB), rows(LANES, TB)],
        out_shape=[sds((S, L, I), F32), sds((S, L, LANES), BF)],
        compiler_params=params(2),
        cost_estimate=pl.CostEstimate(
            flops=2 * S * L * I * D, bytes_accessed=S * L * (4 * I + 2 * D), transcendentals=0
        ),
        name="dnormout",
    )(cotangent, output_weight, od, ou)

    one_state = whole((1, N, I))
    one_sums = pl.BlockSpec((1, 8, Q), lambda s, t: (0, 0, t))
    totals = []
    for one in range(S):
        (part,) = staged(
            sums_kernel, "sums", one,
            [rows(I, Q), rows(2 * N, Q), rows(LANES, Q), one_state, rows(I, Q), rows(I, Q),
             whole((1, I)), whole((2 * LANES, I))],
            (yl, bcc, rc, sins[one], z, dno, og, spread),
            [(one_sums, sds((1, 8, L), F32), False)], None,
        )
        totals.append((part, swap(part)))

    back = lambda t: nc - 1 - t
    back_sums = pl.BlockSpec((1, 8, Q), lambda s, t: (0, 0, nc - 1 - t))
    back_rows = rows(I, Q, back)
    gates, returns = None, []
    for one in range(S):
        gates = staged(
            functools.partial(gate_back_kernel, full=full), "gate_back", one,
            [back_rows, rows(2 * N, Q, back), rows(LANES, Q, back), rows(LANES, Q, back), one_state,
             back_rows, back_rows, back_sums, back_sums, whole((1, I)), whole((2 * LANES, I))],
            (yl, bcc, rc, cum, sins[one], z, dno) + totals[one] + (og, spread),
            [(back_rows, sds((S, L, I), BF), True), (back_rows, sds((S, L, I), BF), True),
             (back_rows, sds((S, L, I), F32), True),
             (chunk4(N, I, back), sds((S, nc, N, I), F32), True),
             (one_state, sds((1, N, I), BF), False)],
            gates, (pltpu.VMEM((N, I), F32),),
        )
        returns.append(gates[-1])
    no, dzr, dy, dc = gates[:4]
    drets = []
    for dsend, dec in zip(returns, decays):
        all_returned = lax.all_gather(dsend, "seq")
        dret = jnp.zeros((1, N, I), F32)
        for p in range(n_seq - 1, 0, -1):
            dret = jnp.where(p > mine, dret * dec[p] + all_returned[p].astype(F32), dret)
        drets.append(dret)

    keep, send_mix, god, gou = pl.pallas_call(
        functools.partial(out_kernel, rank=R),
        grid=grid,
        in_specs=[smem, rows(I, TB), rows(D, TB), rows(D, TB), whole((I, D)), per_seq((LANES, I)),
                  per_seq((LANES, D)), rows(LANES, TB)],
        out_specs=[rows(half, TB), rows(half, TB), per_seq((R, I)), per_seq((R, D))],
        out_shape=[sds((S, L, half), F32), sds((S, L, half), BF), sds((S, R, I), F32), sds((S, R, D), F32)],
        compiler_params=params(2),
        cost_estimate=pl.CostEstimate(
            flops=2 * S * L * I * D, bytes_accessed=S * L * (2 * I + 4 * D), transcendentals=0
        ),
        name="out_proj",
    )(head, no, cotangent, tokens, output_weight, od, ou, blh)

    total = jnp.broadcast_to(rc[:, L - 1 : L], (S, 8, LANES))
    drets[0], keep, send_mix = lax.optimization_barrier((drets[0], keep, send_mix))
    scans = None
    for one in range(S):
        scans = staged(
            functools.partial(scan_back_kernel, heads=H), "scan_back", one,
            [rows(I, Q), rows(2 * N, Q), rows(I, Q), tspec, rows(LANES, Q), rows(LANES, Q),
             rows(LANES, Q), chunk4(8, LANES), chunk4(N, I), one_state, chunk4(N, I), one_state,
             per_seq((8, LANES)), rows(LANES, Q), whole((1, LANES)), whole((1, LANES)), whole((1, I)),
             rows(I, Q), rows(2 * N, Q), whole((LANES, I)), whole((2 * LANES, I))],
            (xc, bcc, dy, cumT, cum, vv, rc, rs, sc, sins[one], dc, drets[one], total, dtr, bias, na,
             skip, slx, slb, emap, spread),
            [(rows(I, Q), sds((S, L, I), F32), True), (rows(2 * N, Q), sds((S, L, 2 * N), F32), True),
             (rows(LANES, Q), sds((S, L, LANES), BF), True)],
            scans, (pltpu.VMEM((LANES, Q), F32),),
        )
    dpx, dpb, ddt = scans
    result = (keep + swap(send_mix).astype(F32)).astype(BF)

    hax = shift(dpx[:, :HALO], "seq", -1)
    hab = shift(dpb[:, :HALO], "seq", -1)
    last = L // HALO - 1
    after = lambda s, t: (s, jnp.minimum((t + 1) * per, last), 0)
    kept, send_grad, giz, gix, gid = pl.pallas_call(
        functools.partial(back_kernel, rank=R),
        grid=grid,
        in_specs=[
            smem, rows(I, TB), pl.BlockSpec((1, HALO, I), after), per_seq((HALO, I)),
            rows(2 * N, TB), pl.BlockSpec((1, HALO, 2 * N), after), per_seq((HALO, 2 * N)),
            rows(I, TB), rows(LANES, TB), rows(D, TB), rows(D, TB), whole((1, D)), rows(LANES, TB),
            whole((D, I)), whole((D, I)), whole((D, 2 * N)), whole((D, LANES)),
            per_seq((LANES, D)), per_seq((LANES, I)), per_seq((LANES, I)),
            whole(conv_x.shape), whole(cvb.shape),
        ],
        out_specs=[rows(half, TB), rows(half, TB), per_seq((R, I)), per_seq((R, I)),
                   per_seq((R, D))],
        out_shape=[sds((S, L, half), F32), sds((S, L, half), F32), sds((S, R, I), F32),
                   sds((S, R, I), F32), sds((S, R, D), F32)],
        scratch_shapes=[pltpu.VMEM((TB + HALO, I), F32), pltpu.VMEM((TB + HALO, 2 * N), F32)],
        compiler_params=params(2),
        name="in_back",
    )(head, dpx, dpx, hax, dpb, dpb, hab, dzr, ddt, tokens, cotangent, gain, lrh, wz, wx, wbc, wst, dn, upz, upx,
      conv_x, cvb)

    grad_tokens = (kept + swap(send_grad)).astype(BF)

    if n_head == 2 and I % (LANES * n_seq) == 0 and D % (2 * LANES * n_seq) == 0 and R % 16 == 0 and n_head * I == 2 * D:
        sums_of = exchange(giz, gix, god, gid, gou, adapter_index, head, NA)
        return (result, grad_tokens) + sums_of

    heads_part = jnp.stack([giz, gix, god], 1)
    shared_part = jnp.stack([gid, gou], 1)
    heads_part = lax.all_gather(lax.psum(heads_part, "seq"), "batch")
    shared_part = lax.all_gather(lax.psum(shared_part, ("seq", "head")), "batch")
    index = lax.all_gather(adapter_index, "batch")
    chosen = (index[:, :, None] == jnp.arange(NA)).astype(F32)

    def table(part):
        return jnp.einsum("bsa,bskri->akri", chosen, part, precision=lax.Precision.HIGHEST)

    heads_sum = table(heads_part)
    shared_sum = table(shared_part)
    grad_in_up = jnp.swapaxes(heads_sum[:, :2], 1, 2)
    grad_out_down = jnp.swapaxes(heads_sum[:, 2], 1, 2)
    grad_in_down = jnp.swapaxes(shared_sum[:, 0], 1, 2)
    grad_out_up = shared_sum[:, 1]
    return (result, grad_tokens, grad_in_down, grad_in_up, grad_out_down, grad_out_up)


def solution(mesh):
    in_specs = (
        P("batch", "seq", None),
        P("batch", "seq", None),
        P("batch"),
        P(),
        P(None, None, "head"),
        P(None, None, "head"),
        P(None, "head"),
        P(None, "head"),
        P(None, None, "head"),
        P("head"),
        P("head"),
        P("head"),
        P("head"),
        P("head", None),
        P(),
        P(None, None, None, "head"),
        P(None, "head", None),
        P(),
    )
    out_specs = (
        P("batch", "seq", "head"),
        P("batch", "seq", "head"),
        P(),
        P(None, None, None, "head"),
        P(None, "head", None),
        P(),
    )
    return jax.shard_map(local, mesh=mesh, in_specs=in_specs, out_specs=out_specs, check_vma=False)
```

```python
import functools

import jax
import jax.numpy as jnp
from jax import lax
from jax.experimental import pallas as pl
from jax.experimental.pallas import tpu as pltpu
from jax.sharding import PartitionSpec as P

EPSILON = 1e-05
LOG2E = 1.4426950408889634
CHUNK = 128
LANES = 128
HALO = 16
BF = jnp.bfloat16
F32 = jnp.float32
VMEM_LIMIT = 60 * 1024 * 1024


def mm(a, b):
    return lax.dot_general(a, b, (((1,), (0,)), ((), ())), preferred_element_type=F32)


def nt(a, b):
    return lax.dot_general(a, b, (((1,), (1,)), ((), ())), preferred_element_type=F32)


def tn(a, b):
    return lax.dot_general(a, b, (((0,), (0,)), ((), ())), preferred_element_type=F32)


def lane_of(shape):
    return lax.broadcasted_iota(jnp.int32, shape, len(shape) - 1)


def row_of(shape):
    return lax.broadcasted_iota(jnp.int32, shape, len(shape) - 2)


def split_dup(v, rank):
    high = v.astype(BF)
    rest = (v - high.astype(F32)).astype(BF)
    return jnp.where(lane_of(v.shape) < rank, high, rest)


def fold(v, rank):
    return v[:rank] + v[rank : 2 * rank]


def expand(v, spread):
    high = v.astype(BF)
    rest = (v - high.astype(F32)).astype(BF)
    return mm(jnp.concatenate([high, rest], 1), spread)


def parts(v):
    high = v.astype(BF)
    return high, (v - high.astype(F32)).astype(BF)


def gather(v, emap):
    high, rest = parts(v)
    return nt(high, emap) + nt(rest, emap)


def both(product, a, b):
    if not isinstance(a, tuple):
        return product(a, b[0]) + product(a, b[1])
    if not isinstance(b, tuple):
        return product(a[0], b) + product(a[1], b)
    return product(a[0], b[0]) + product(a[0], b[1]) + product(a[1], b[0])


def paired(ws):
    return tuple(jnp.concatenate([ws[0][i], ws[1][i]], 1) for i in range(2))


def tri_sum(tri, v):
    a = v.astype(BF)
    r = v - a.astype(F32)
    b = r.astype(BF)
    c = (r - b.astype(F32)).astype(BF)
    w = v.shape[1]
    out = mm(tri, jnp.concatenate([a, b, c], 1))
    return out[:, :w] + out[:, w : 2 * w] + out[:, 2 * w :]


def sigm(v):
    return 0.5 * jnp.tanh(0.5 * v) + 0.5


def softplus(v):
    return jnp.maximum(v, 0.0) + jnp.log(1.0 + jnp.exp(-jnp.abs(v)))


def params(n):
    return pltpu.CompilerParams(
        dimension_semantics=("arbitrary",) * n, vmem_limit_bytes=VMEM_LIMIT
    )


def halves(v, h):
    w = v.shape[1] // 2
    lo, hi = v[:, :w], v[:, w:]
    return jnp.where(h == 0, lo, hi), jnp.where(h == 0, hi, lo)


def unweave_kernel(w, even, odd):
    n = 2 * w.shape[0]
    r = row_of((n, n))
    c = lane_of((n, n))
    m = (c == jnp.where(r < n // 2, 2 * r, 2 * r - n + 1)).astype(BF)
    out = mm(m, w[...].reshape(n, w.shape[2])).astype(BF)
    even[...] = out[: n // 2]
    odd[...] = out[n // 2 :]


def front_kernel(
    tok, prev, halo, gain, wz, wx, wbc, wst, dn, upz, upx, cvx, cvb,
    z, xc, slx, bcc, slb, dtr, lrh, xs, bs, *, rank,
):
    t = pl.program_id(1)
    rows = tok.shape[1]

    def normed(v):
        f = v.astype(F32)
        scale = lax.rsqrt(jnp.mean(f * f, -1, keepdims=True) + EPSILON)
        return (f * scale * gain[...]).astype(BF)

    before = jnp.where(t == 0, halo[0], prev[0])
    ext = jnp.concatenate([normed(before), normed(tok[0])], 0)
    main = ext[HALO:]
    low = split_dup(nt(ext, dn[0]), rank)
    lrh[0] = low[HALO:]
    z[0] = (mm(main, wz[...]) + mm(low[HALO:], upz[0])).astype(BF)
    dtr[0] = mm(main, wst[...]).astype(BF).astype(F32)

    def conv(raw, keep, taps, act, slope):
        keep[...] = raw.astype(BF).astype(F32)
        pre = taps[4:5]
        for k in range(4):
            pre = pre + taps[k : k + 1] * keep[HALO - 3 + k : HALO - 3 + k + rows]
        s = sigm(pre)
        a = pre * s
        act[0] = a.astype(BF)
        slope[0] = s + a * (1.0 - s)

    conv(mm(ext, wx[...]) + mm(low, upx[0]), xs, cvx[...], xc, slx)
    conv(mm(ext, wbc[...]), bs, cvb[...], bcc, slb)


def state_kernel(dtr, xc, bcc, bias, na, spread, cum, vv, rc, cumT, vT, rs, sc, send, st, run):
    c = pl.program_id(1)
    q = CHUNK
    n = bcc.shape[2] // 2

    @pl.when(c == 0)
    def _():
        st[...] = jnp.zeros_like(st)
        run[...] = jnp.zeros_like(run)

    dt = softplus(dtr[0] + bias[...])
    tri = (row_of((q, q)) >= lane_of((q, q))).astype(BF)
    cm = tri_sum(tri, dt * na[...])
    v = cm - jnp.log2(dt)
    cum[0] = cm
    vv[0] = v
    rc[0] = cm + run[0:1]
    hr = cumT.shape[1]
    cumT[0] = jnp.transpose(cm)[:hr]
    vT[0] = jnp.transpose(v)[:hr]
    rs[0, 0] = run[...]
    sc[0, 0] = st[...]
    last = cm[q - 1 : q]
    w = expand(jnp.exp2(last - v), spread[...])
    wx = parts(w * xc[0].astype(F32))
    dec = expand(jnp.exp2(jnp.broadcast_to(last, (8, LANES))), spread[...])[0:1]
    st[...] = dec * st[...] + both(tn, bcc[0][:, :n], wx)
    run[...] = run[...] + last

    @pl.when(c == pl.num_programs(1) - 1)
    def _():
        send[0, :n] = st[...].astype(BF)
        total = expand(jnp.exp2(run[...]), spread[...])
        high = total.astype(BF)
        rest = (total - high.astype(F32)).astype(BF)
        send[0, n:] = jnp.concatenate([high, rest], 0)


def intra_kernel(xc, bcc, cum, vT, sc, skip, spread, y, *, heads):
    q = CHUNK
    n = bcc.shape[2] // 2
    b = bcc[0][:, :n]
    c = bcc[0][:, n:]
    scores = nt(c, b)
    allowed = row_of((q, q)) >= lane_of((q, q))
    cm = cum[0]
    e = expand(jnp.exp2(cm), spread[...])
    y[0] = both(mm, c, parts(sc[0, 0])) * e + skip[...] * xc[0].astype(F32)
    first = lane_of((q, LANES)) < LANES // 2
    for j in range(heads // 2):
        ws = []
        for h in (2 * j, 2 * j + 1):
            d = cm[:, h : h + 1] - vT[0, h : h + 1, :]
            ws.append(parts(jnp.exp2(jnp.where(allowed, d, -jnp.inf)) * scores))
        cols = slice(j * LANES, (j + 1) * LANES)
        xp = xc[0, :, cols]
        zero = jnp.zeros_like(xp)
        xbd = jnp.concatenate([jnp.where(first, xp, zero), jnp.where(first, zero, xp)], 0)
        y[0, :, cols] += both(mm, paired(ws), xbd)


def dnormout_kernel(g, wo, od, ou, dno, blh, *, rank):
    low = split_dup(nt(g[0], ou[0]), rank)
    blh[0] = low
    dno[0] = nt(g[0], wo[...]) + mm(low, od[0])


def gated_of(yl, bcc, rc, sin, z, spread):
    n = bcc.shape[2] // 2
    y = yl[0] + expand(jnp.exp2(rc[0]), spread[...]) * both(mm, bcc[0][:, n:], parts(sin[0]))
    gate = z[0].astype(F32)
    s = sigm(gate)
    return y, gate, s


def sums_kernel(place, every, yl, bcc, rc, z, dno, og, spread, sums, sin, decays):
    n = sin.shape[1]

    @pl.when(pl.program_id(1) == 0)
    def _():
        state = jnp.zeros(sin.shape[1:], F32)
        for p in range(every.shape[0]):
            dec = every[p, 0, n : n + 1].astype(F32) + every[p, 0, n + 8 : n + 9].astype(F32)
            decays[p : p + 1] = dec
            if p < every.shape[0] - 1:
                state = jnp.where(p < place[0], state * dec + every[p, 0, :n].astype(F32), state)
        sin[0] = state

    y, gate, s = gated_of(yl, bcc, rc, sin, z, spread)
    gated = y * (gate * s)
    sq = jnp.sum(gated * gated, -1, keepdims=True)
    tot = jnp.sum(dno[0] * og[...] * gated, -1, keepdims=True)
    both_sums = jnp.where(lane_of((sq.shape[0], LANES)) == 0, sq, tot)
    sums[0] = jnp.transpose(both_sums)[:8]


def gate_back_kernel(
    yl, bcc, rc, cum, sin, z, dno, mine, other, og, spread, no, dzr, dy, dc, send, dst, *, full
):
    step = pl.program_id(1)
    q = CHUNK
    n = bcc.shape[2] // 2

    @pl.when(step == 0)
    def _():
        dst[...] = jnp.zeros_like(dst)

    y, gate, s = gated_of(yl, bcc, rc, sin, z, spread)
    act = gate * s
    gated = y * act
    sums = mine[0] + other[0]
    sums = jnp.transpose(jnp.concatenate([sums, jnp.zeros((LANES - 8, q), F32)], 0))
    r = lax.rsqrt(sums[:, 0:1] / full + EPSILON)
    k = r * r * r * (sums[:, 1:2] / full)
    no[0] = (gated * r * og[...]).astype(BF)
    dg = r * (og[...] * dno[0]) - gated * k
    dzr[0] = (dg * y * (s + act * (1.0 - s))).astype(BF)
    dyv = dg * act
    dy[0] = dyv
    dc[0, 0] = dst[...]
    e = expand(jnp.exp2(cum[0]), spread[...])
    dst[...] = e[q - 1 : q] * dst[...] + both(tn, bcc[0][:, n:], parts(e * dyv))

    @pl.when(step == pl.num_programs(1) - 1)
    def _():
        send[0] = dst[...].astype(BF)


def out_kernel(head, no, g, tok, wo, od, ou, blh, keep, send, god, gou, *, rank):
    t = pl.program_id(1)

    @pl.when(t == 0)
    def _():
        god[...] = jnp.zeros_like(god)
        gou[...] = jnp.zeros_like(gou)

    low = split_dup(nt(no[0], od[0]), rank)
    own, other = halves(mm(no[0], wo[...]) + mm(low, ou[0]), head[0])
    keep[0] = own + halves(tok[0].astype(F32), head[0])[0]
    send[0] = other.astype(BF)
    god[0] += fold(tn(blh[0], no[0]), rank)
    gou[0] += fold(tn(low, g[0]), rank)


def scan_back_kernel(
    place, every, decays, xc, bcc, dy, cumT, cum, vv, rc, rs, sc, sin, dc, total, dtr, bias, na, skip,
    slx, slb, emap, spread, dpx, dpb, ddt, rowq, dret, *, heads,
):
    @pl.when(pl.program_id(1) == 0)
    def _():
        state = jnp.zeros(dret.shape, F32)
        for p in range(every.shape[0] - 1, 0, -1):
            state = jnp.where(
                p > place[0], state * decays[p : p + 1] + every[p, 0].astype(F32), state
            )
        dret[...] = state

    q = CHUNK
    n = bcc.shape[2] // 2
    b = bcc[0][:, :n]
    c = bcc[0][:, n:]
    sT = nt(b, c)
    allowed = lane_of((q, q)) >= row_of((q, q))
    sT = jnp.where(allowed, sT, 0.0)
    cm = cum[0]
    v = vv[0]
    last = cm[q - 1 : q]
    first = lane_of((q, LANES)) < LANES // 2
    lanes = lane_of((q, LANES))
    rowq[...] = jnp.zeros_like(rowq)
    ds = jnp.zeros((q, q), F32)
    colq = jnp.zeros((q, LANES), F32)
    head8 = jnp.concatenate(
        [rs[0, 0][0:1], total[0][0:1] - rc[0][q - 1 : q], last, jnp.zeros((5, LANES), F32)], 0
    )
    decs = expand(jnp.exp2(head8), spread[...])
    s_in = sc[0, 0] + decs[0:1] * sin[0]
    d_out = dc[0, 0] + decs[1:2] * dret[...]
    s_two = parts(s_in)
    d_two = parts(d_out)
    x = xc[0].astype(F32)
    dyf = dy[0]
    e = expand(jnp.exp2(cm), spread[...])
    w = expand(jnp.exp2(last - v), spread[...])
    ed = e * dyf
    carried = both(mm, c, s_two)
    wbd = w * both(mm, b, d_two)
    wx = w * x
    up = gather(ed * carried, emap[...])
    vs = gather(x * wbd, emap[...])
    cross = gather(d_out * s_in, emap[...])
    crossed = jnp.sum(cross, 0, keepdims=True) * jnp.exp2(last)
    d_c = both(nt, parts(ed), s_two)
    d_b = both(nt, parts(wx), d_two)
    slope = slx[0]
    base = wbd + skip[...] * dyf
    for j in range(heads // 2):
        cols = slice(j * LANES, (j + 1) * LANES)
        xp = xc[0, :, cols]
        dbd = []
        for dp in parts(dyf[:, cols]):
            zero = jnp.zeros_like(dp)
            dbd.append(jnp.concatenate([jnp.where(first, dp, zero), jnp.where(first, zero, dp)], 0))
        dbd = tuple(dbd)
        dw = both(nt, xp, dbd)
        ws = []
        for i, h in enumerate((2 * j, 2 * j + 1)):
            d = cumT[0, h : h + 1, :] - v[:, h : h + 1]
            ex = jnp.exp2(jnp.where(allowed, d, -jnp.inf))
            ws.append(parts(ex * sT))
            dwe = dw[:, i * q : (i + 1) * q] * ex
            ds = ds + dwe
            qm = dwe * sT
            rowq[h : h + 1, :] = jnp.sum(qm, 0, keepdims=True)
            colq = jnp.where(lanes == h, jnp.sum(qm, 1, keepdims=True), colq)
        dx = both(mm, paired(ws), dbd) + base[:, cols]
        dpx[0, :, cols] = dx * slope[:, cols]
    ds_two = parts(ds)
    d_b = d_b + both(mm, ds_two, c)
    d_c = d_c + both(tn, ds_two, b)
    dpb[0] = jnp.concatenate([d_b, d_c], 1) * slb[0]
    rq = jnp.transpose(rowq[...])
    upper = (row_of((q, q)) <= lane_of((q, q))).astype(BF)
    lower = (row_of((q, q)) > lane_of((q, q))).astype(BF)
    dlog = tri_sum(upper, rq - colq + up) + tri_sum(lower, vs) + crossed
    raw = dtr[0] + bias[...]
    dt = softplus(raw)
    sg = jax.nn.sigmoid(raw)
    ratio = sg / jnp.maximum(dt, 1e-37)
    out = (colq + vs) * ratio + dlog * (na[...] * (1.0 / LOG2E)) * sg
    ddt[0] = jnp.where(lanes < heads, out, 0.0).astype(BF)


def back_kernel(
    head, dpx, nxx, hax, dpb, nxb, hab, dzr, ddt, tok, cot, gain, lrh, wz, wx, wbc, wst, dn, upz, upx, cvx, cvb,
    kept, send, giz, gix, gid, xs, bs, *, rank,
):
    t = pl.program_id(1)
    rows = tok.shape[1]
    end = t == pl.num_programs(1) - 1

    @pl.when(t == 0)
    def _():
        giz[...] = jnp.zeros_like(giz)
        gix[...] = jnp.zeros_like(gix)
        gid[...] = jnp.zeros_like(gid)

    def conv(tile, nxt, halo, keep, taps):
        keep[:rows] = tile[0]
        keep[rows:] = jnp.where(end, halo[0], nxt[0])
        out = taps[3:4] * keep[:rows]
        for k in range(3):
            out = out + taps[k : k + 1] * keep[3 - k : 3 - k + rows]
        return out.astype(BF)

    f = tok[0].astype(F32)
    scale = lax.rsqrt(jnp.mean(f * f, -1, keepdims=True) + EPSILON)
    nm = (f * scale * gain[...]).astype(BF)
    dz = dzr[0]
    dx = conv(dpx, nxx, hax, xs, cvx[...])
    db = conv(dpb, nxb, hab, bs, cvb[...])
    low = split_dup(nt(dz, upz[0]) + nt(dx, upx[0]), rank)
    out = nt(dz, wz[...]) + nt(dx, wx[...]) + nt(db, wbc[...]) + nt(ddt[0], wst[...])
    out = out + mm(low, dn[0])
    dg = out * gain[...]
    stat = jnp.sum(dg * f, -1, keepdims=True) / f.shape[1]
    own, other = halves(scale * dg - f * (scale * scale * scale * stat), head[0])
    kept[0] = own + halves(cot[0].astype(F32), head[0])[0]
    send[0] = other
    giz[0] += fold(tn(lrh[0], dz), rank)
    gix[0] += fold(tn(lrh[0], dx), rank)
    gid[0] += fold(tn(low, nm), rank)


def shift(x, axis, by):
    count = lax.axis_size(axis)
    return lax.ppermute(x, axis, [(i, i + by) for i in range(count) if 0 <= i + by < count])


def exchange_kernel(
    giz, gix, god, gid, gou, idx, out, pair, index, low, got, got2, s1, r1, s2, r2, s3, r3, s4, r4, s5, r5,
    s6, r6,
):
    nz, nb = lax.axis_size("seq"), lax.axis_size("batch")
    z, h, b = lax.axis_index("seq"), lax.axis_index("head"), lax.axis_index("batch")
    rows = giz.shape[0]
    w = giz.shape[1] // nz
    w2 = gid.shape[1] // (2 * nz)

    def plus(i, by, n):
        return lax.rem(i + by, n)

    def cut(p):
        return pl.ds(pl.multiple_of(p * w, w), w)

    def cut2(p, q):
        return pl.ds(pl.multiple_of((q * nz + p) * w2, w2), w2)

    def copy(src, dst, send, recv, **where):
        return pltpu.make_async_remote_copy(
            src_ref=src, dst_ref=dst, send_sem=send, recv_sem=recv, device_id=where,
            device_id_type=pl.DeviceIdType.MESH,
        )

    for k, ref in enumerate((giz, gix, god, gid, gou)):
        low[k] = ref[...].astype(BF)
    barrier = pltpu.get_barrier_semaphore()
    pairs = [(d, e) for d in range(nz) for e in range(2) if d or e]
    for d, e in pairs:
        pl.semaphore_signal(
            barrier, inc=1, device_id={"seq": plus(z, d, nz), "head": plus(h, e, 2)},
            device_id_type=pl.DeviceIdType.MESH,
        )
    for f in range(1, nb):
        pl.semaphore_signal(
            barrier, inc=1, device_id={"batch": plus(b, f, nb)},
            device_id_type=pl.DeviceIdType.MESH,
        )
    pl.semaphore_wait(barrier, len(pairs) + nb - 1)

    first = []
    for d in range(1, nz):
        p = plus(z, d, nz)
        for k in range(3):
            first.append(copy(low.at[k, :, cut(p)], got.at[k, d], s1.at[k, d], r1.at[k, d], seq=p))
    for i, (d, e) in enumerate(pairs):
        p, q = plus(z, d, nz), plus(h, e, 2)
        for k in range(2):
            first.append(
                copy(low.at[3 + k, :, cut2(p, q)], got2.at[k, i], s2.at[k, i], r2.at[k, i], seq=p, head=q)
            )
    for f in range(1, nb):
        first.append(copy(idx, index.at[b], s3.at[f], r3.at[f], batch=plus(b, f, nb)))
    for c in first:
        c.start()
    index[b] = idx[...]
    for c in first:
        c.wait_recv()
    for k, ref in enumerate((giz, gix, god)):
        total = ref[:, cut(z)]
        for d in range(1, nz):
            total = total + got[k, d].astype(F32)
        out[b, z, k * rows : (k + 1) * rows] = total.astype(BF)
    parts = []
    for k, ref in enumerate((gid, gou)):
        total = ref[:, cut2(z, h)]
        for i in range(len(pairs)):
            total = total + got2[k, i].astype(F32)
        parts.append(total.astype(BF))
    out[b, z, 3 * rows :] = jnp.concatenate(parts, 1)
    for c in first:
        c.wait_send()

    sent = []

    def ship(k, src):
        for f in range(1, nb):
            c = copy(src, src, s5.at[k, f], r5.at[k, f], batch=plus(b, f, nb))
            c.start()
            sent.append(c)

    own = out.at[b, z]
    for d in range(1, nz):
        c = copy(own, own, s4.at[d], r4.at[d], seq=plus(z, d, nz))
        c.start()
        sent.append(c)
    ship(0, own)
    for d in range(1, nz):
        there = out.at[b, plus(z, nz - d, nz)]
        copy(there, there, s4.at[d], r4.at[d], seq=plus(z, d, nz)).wait_recv()
        ship(d, there)
    for d in range(nz):
        for f in range(1, nb):
            there = out.at[plus(b, nb - f, nb), plus(z, nz - d, nz)]
            copy(there, there, s5.at[d, f], r5.at[d, f], batch=plus(b, f, nb)).wait_recv()
    for c in sent:
        c.wait_send()
    last = copy(out.at[:, :, pl.ds(3 * rows, rows)], pair, s6, r6, head=plus(h, 1, 2))
    last.start()
    last.wait()


def table_kernel(idx, head, out, pair, up, od, idn, oup, *, seqs):
    nb, nz, _, w = out.shape
    rows = pair.shape[2]
    rank = od.shape[1]
    w2 = w // 2
    h = head[0]
    for ref in (up, od, idn, oup):
        ref[...] = jnp.zeros_like(ref)
    for b in range(nb):
        for s in range(seqs):
            a = idx[b * seqs + s]
            for z in range(nz):

                def part(ref, k):
                    return ref[b, z, k * rows + s * rank : k * rows + (s + 1) * rank].astype(F32)

                cols = slice(z * w, (z + 1) * w)
                up[a, 0, :, cols] += part(out, 0)
                up[a, 1, :, cols] += part(out, 1)
                od[a, :, cols] += part(out, 2)
                mine, other = part(out, 3), part(pair, 0)
                for q, v in ((0, jnp.where(h == 0, mine, other)), (1, jnp.where(h == 0, other, mine))):
                    cols = slice((q * nz + z) * w2, (q * nz + z + 1) * w2)
                    idn[a, :, cols] += v[:, :w2]
                    oup[a, :, cols] += v[:, w2:]


def exchange(giz, gix, god, gid, gou, adapter_index, head, adapters):
    S, R, I = giz.shape
    D = gid.shape[2]
    nz, nb = lax.axis_size("seq"), lax.axis_size("batch")
    rows = S * R
    w, w2 = I // nz, D // (2 * nz)
    if 2 * w2 != w:
        raise ValueError("widths differ")
    sds = jax.ShapeDtypeStruct
    dma = pltpu.SemaphoreType.DMA
    vmem = pl.BlockSpec(memory_space=pltpu.VMEM)
    smem = pl.BlockSpec(memory_space=pltpu.SMEM)
    flat = [v.reshape(rows, v.shape[2]) for v in (giz, gix, god, gid, gou)]
    idx = jnp.zeros((8, LANES), F32).at[0, :S].set(adapter_index.astype(F32))
    others = 2 * nz - 1
    out, pair, index = pl.pallas_call(
        exchange_kernel,
        in_specs=[vmem] * 6,
        out_specs=[vmem] * 3,
        out_shape=[sds((nb, nz, 4 * rows, w), BF), sds((nb, nz, rows, w), BF), sds((nb, 8, LANES), F32)],
        scratch_shapes=[
            pltpu.VMEM((5, rows, I), BF), pltpu.VMEM((3, nz, rows, w), BF),
            pltpu.VMEM((2, others, rows, w2), BF),
            dma((3, nz)), dma((3, nz)), dma((2, others)), dma((2, others)), dma((nb,)), dma((nb,)),
            dma((nz,)), dma((nz,)), dma((nz, nb)), dma((nz, nb)), dma, dma,
        ],
        compiler_params=pltpu.CompilerParams(collective_id=0, has_side_effects=True),
        name="exchange",
    )(*flat, idx)
    where = index[:, 0, :S].reshape(nb * S).astype(jnp.int32)
    up, od, idn, oup = pl.pallas_call(
        functools.partial(table_kernel, seqs=S),
        in_specs=[smem, smem, vmem, vmem],
        out_specs=[vmem] * 4,
        out_shape=[sds((adapters, 2, R, I), F32), sds((adapters, R, I), F32),
                   sds((adapters, R, D), F32), sds((adapters, R, D), F32)],
        compiler_params=pltpu.CompilerParams(vmem_limit_bytes=VMEM_LIMIT),
        name="tables",
    )(where, head, out, pair)
    return (jnp.swapaxes(idn, 1, 2), jnp.swapaxes(up, 1, 2), jnp.swapaxes(od, 1, 2), oup)


def local(
    tokens, cotangent, adapter_index, norm_gain, gate_input_weight, bc_weight, step_weight,
    conv_x, conv_bc, dt_bias, a_log, skip_gain, out_gain, output_weight,
    in_down, in_up, out_down, out_up,
):
    S, L, D = tokens.shape
    H = dt_bias.shape[0]
    I = output_weight.shape[0]
    N = bc_weight.shape[2] * lax.axis_size("head")
    NA = in_down.shape[0]
    R = in_down.shape[2]
    hp = I // H
    n_seq = lax.axis_size("seq")
    n_head = lax.axis_size("head")
    full = float(I * n_head)
    TB = min(256, L)
    half = D // n_head

    def swap(v):
        return lax.ppermute(v, "head", [(0, 1), (1, 0)])

    Q = CHUNK
    nc = L // Q
    HR = max(8, -(-H // 8) * 8)
    sds = jax.ShapeDtypeStruct

    UW = min(256, 2 * D)
    wz, wx = pl.pallas_call(
        unweave_kernel,
        grid=(2 * D // UW,),
        in_specs=[pl.BlockSpec((UW // 2, 2, I), lambda t: (t, 0, 0))],
        out_specs=[pl.BlockSpec((UW // 2, I), lambda t: (t, 0))] * 2,
        out_shape=[sds((D, I), BF)] * 2,
        compiler_params=params(1),
        name="unweave",
    )(gate_input_weight)
    head = lax.axis_index("head").astype(jnp.int32)[None]
    smem = pl.BlockSpec(memory_space=pltpu.SMEM)
    wbc = lax.all_gather(bc_weight, "head", axis=2, tiled=True).reshape(D, 2 * N)
    cvb = lax.all_gather(conv_bc, "head", axis=2, tiled=True).reshape(conv_bc.shape[0], 2 * N)
    wst = jnp.pad(step_weight, ((0, 0), (0, LANES - H)))
    onehot = (adapter_index[:, None] == jnp.arange(NA)[None, :]).astype(BF)

    def stack(rows):
        return jnp.concatenate(
            [rows, rows, jnp.zeros((S, LANES - 2 * R, rows.shape[2]), BF)], 1
        )

    def pick(spec, table):
        return jnp.einsum(spec, onehot, table, preferred_element_type=F32).astype(BF)

    dn = stack(pick("sa,adr->srd", in_down))
    up = pick("sa,arki->skri", in_up)
    upz = stack(up[:, 0])
    upx = stack(up[:, 1])
    od = stack(pick("sa,air->sri", out_down))
    ou = stack(pick("sa,ard->srd", out_up))
    emap = (jnp.arange(LANES)[:, None] == (jnp.arange(I) // hp)[None, :]).astype(BF)
    spread = jnp.concatenate([emap, emap], 0)

    def lanes(v):
        return jnp.pad(v, (0, LANES - H))[None]

    bias = lanes(dt_bias)
    na = lanes(-jnp.exp(a_log) * LOG2E)
    skip = jnp.repeat(skip_gain, hp)[None]
    gain = norm_gain[None]
    og = out_gain[None]

    def rows(width, tb, order=None):
        f = (lambda s, t: (s, t, 0)) if order is None else (lambda s, t: (s, order(t), 0))
        return pl.BlockSpec((1, tb, width), f)

    def whole(shape):
        return pl.BlockSpec(shape, lambda s, t: (0,) * len(shape))

    def per_seq(shape):
        return pl.BlockSpec((1,) + shape, lambda s, t: (s,) + (0,) * len(shape))

    def chunk4(a, b_, order=None):
        f = (lambda s, t: (s, t, 0, 0)) if order is None else (lambda s, t: (s, order(t), 0, 0))
        return pl.BlockSpec((1, 1, a, b_), f)

    def staged(kernel, name, one, in_specs, args, outs, prev, scratch=()):
        def at(spec):
            if spec.index_map is None:
                return spec
            return pl.BlockSpec(spec.block_shape, lambda s, t: spec.index_map(one, t))

        shared = [i for i, o in enumerate(outs) if o[2]] if prev else []
        n = len(args)

        def body(*refs):
            kernel(*refs[:n], *refs[n + len(shared) :])

        return pl.pallas_call(
            body,
            grid=(1, nc),
            in_specs=[at(v) for v in in_specs] + [pl.BlockSpec(memory_space=pl.ANY)] * len(shared),
            out_specs=[at(o[0]) for o in outs],
            out_shape=[o[1] for o in outs],
            scratch_shapes=list(scratch),
            input_output_aliases={n + i: k for i, k in enumerate(shared)},
            compiler_params=params(2),
            name=name,
        )(*args, *[prev[k] for k in shared])

    halo = shift(tokens[:, L - HALO :], "seq", 1)
    per = TB // HALO
    grid = (S, L // TB)
    z, xc, slx, bcc, slb, dtr, lrh = pl.pallas_call(
        functools.partial(front_kernel, rank=R),
        grid=grid,
        in_specs=[
            rows(D, TB),
            pl.BlockSpec((1, HALO, D), lambda s, t: (s, jnp.maximum(t * per - 1, 0), 0)),
            per_seq((HALO, D)),
            whole((1, D)), whole((D, I)), whole((D, I)), whole((D, 2 * N)), whole((D, LANES)),
            per_seq((LANES, D)), per_seq((LANES, I)), per_seq((LANES, I)),
            whole(conv_x.shape), whole(cvb.shape),
        ],
        out_specs=[rows(I, TB), rows(I, TB), rows(I, TB), rows(2 * N, TB), rows(2 * N, TB),
                   rows(LANES, TB), rows(LANES, TB)],
        out_shape=[sds((S, L, I), BF), sds((S, L, I), BF), sds((S, L, I), F32),
                   sds((S, L, 2 * N), BF), sds((S, L, 2 * N), F32),
                   sds((S, L, LANES), F32), sds((S, L, LANES), BF)],
        scratch_shapes=[pltpu.VMEM((TB + HALO, I), F32), pltpu.VMEM((TB + HALO, 2 * N), F32)],
        compiler_params=params(2),
        name="front",
    )(tokens, tokens, halo, gain, wz, wx, wbc, wst, dn, upz, upx, conv_x, cvb)

    cgrid = (S, nc)
    tspec = pl.BlockSpec((1, HR, Q), lambda s, t: (s, 0, t))
    lane_rows = (rows(LANES, Q), sds((S, L, LANES), F32), True)
    head_rows = (tspec, sds((S, HR, L), F32), True)
    state_outs = [
        lane_rows, lane_rows, lane_rows, head_rows, head_rows,
        (chunk4(8, LANES), sds((S, nc, 8, LANES), F32), True),
        (chunk4(N, I), sds((S, nc, N, I), F32), True),
        (whole((1, N + 16, I)), sds((1, N + 16, I), BF), False),
    ]
    mine = lax.axis_index("seq")
    states, sends = None, []
    for one in range(S):
        states = staged(
            state_kernel, "states", one,
            [rows(LANES, Q), rows(I, Q), rows(2 * N, Q), whole((1, LANES)), whole((1, LANES)),
             whole((2 * LANES, I))],
            (dtr, xc, bcc, bias, na, spread), state_outs, states,
            (pltpu.VMEM((N, I), F32), pltpu.VMEM((8, LANES), F32)),
        )
        sends.append(states[-1])
    cum, vv, rc, cumT, vT, rs, sc = states[:7]
    place = mine.astype(jnp.int32)[None]
    every = [lax.all_gather(send, "seq") for send in sends]

    yl = pl.pallas_call(
        functools.partial(intra_kernel, heads=H),
        grid=cgrid,
        in_specs=[rows(I, Q), rows(2 * N, Q), rows(LANES, Q), tspec, chunk4(N, I), whole((1, I)),
                  whole((2 * LANES, I))],
        out_specs=rows(I, Q),
        out_shape=sds((S, L, I), F32),
        compiler_params=params(2),
        cost_estimate=pl.CostEstimate(
            flops=S * L * I * 8 * Q, bytes_accessed=S * L * I * 12, transcendentals=S * L * H * Q
        ),
        name="intra",
    )(xc, bcc, cum, vT, sc, skip, spread)

    dno, blh = pl.pallas_call(
        functools.partial(dnormout_kernel, rank=R),
        grid=grid,
        in_specs=[rows(D, TB), whole((I, D)), per_seq((LANES, I)), per_seq((LANES, D))],
        out_specs=[rows(I, TB), rows(LANES, TB)],
        out_shape=[sds((S, L, I), F32), sds((S, L, LANES), BF)],
        compiler_params=params(2),
        cost_estimate=pl.CostEstimate(
            flops=2 * S * L * I * D, bytes_accessed=S * L * (4 * I + 2 * D), transcendentals=0
        ),
        name="dnormout",
    )(cotangent, output_weight, od, ou)

    one_state = whole((1, N, I))
    one_sums = pl.BlockSpec((1, 8, Q), lambda s, t: (0, 0, t))
    totals, sins, decays = [], [], []
    for one in range(S):
        part, sin, dec = staged(
            sums_kernel, "sums", one,
            [smem, whole((n_seq, 1, N + 16, I)), rows(I, Q), rows(2 * N, Q), rows(LANES, Q), rows(I, Q),
             rows(I, Q), whole((1, I)), whole((2 * LANES, I))],
            (place, every[one], yl, bcc, rc, z, dno, og, spread),
            [(one_sums, sds((1, 8, L), F32), False), (one_state, sds((1, N, I), F32), False),
             (whole((n_seq, I)), sds((n_seq, I), F32), False)], None,
        )
        totals.append((part, swap(part)))
        sins.append(sin)
        decays.append(dec)

    back = lambda t: nc - 1 - t
    back_sums = pl.BlockSpec((1, 8, Q), lambda s, t: (0, 0, nc - 1 - t))
    back_rows = rows(I, Q, back)
    gates, returns = None, []
    for one in range(S):
        gates = staged(
            functools.partial(gate_back_kernel, full=full), "gate_back", one,
            [back_rows, rows(2 * N, Q, back), rows(LANES, Q, back), rows(LANES, Q, back), one_state,
             back_rows, back_rows, back_sums, back_sums, whole((1, I)), whole((2 * LANES, I))],
            (yl, bcc, rc, cum, sins[one], z, dno) + totals[one] + (og, spread),
            [(back_rows, sds((S, L, I), BF), True), (back_rows, sds((S, L, I), BF), True),
             (back_rows, sds((S, L, I), F32), True),
             (chunk4(N, I, back), sds((S, nc, N, I), F32), True),
             (one_state, sds((1, N, I), BF), False)],
            gates, (pltpu.VMEM((N, I), F32),),
        )
        returns.append(gates[-1])
    no, dzr, dy, dc = gates[:4]
    returned = [lax.all_gather(dsend, "seq") for dsend in returns]

    total = jnp.broadcast_to(rc[:, L - 1 : L], (S, 8, LANES))
    scans = None
    for one in range(S):
        scans = staged(
            functools.partial(scan_back_kernel, heads=H), "scan_back", one,
            [smem, whole((n_seq, 1, N, I)), whole((n_seq, I)), rows(I, Q), rows(2 * N, Q), rows(I, Q),
             tspec, rows(LANES, Q), rows(LANES, Q), rows(LANES, Q), chunk4(8, LANES), chunk4(N, I),
             one_state, chunk4(N, I),
             per_seq((8, LANES)), rows(LANES, Q), whole((1, LANES)), whole((1, LANES)), whole((1, I)),
             rows(I, Q), rows(2 * N, Q), whole((LANES, I)), whole((2 * LANES, I))],
            (place, returned[one], decays[one], xc, bcc, dy, cumT, cum, vv, rc, rs, sc, sins[one], dc, total, dtr, bias, na,
             skip, slx, slb, emap, spread),
            [(rows(I, Q), sds((S, L, I), F32), True), (rows(2 * N, Q), sds((S, L, 2 * N), F32), True),
             (rows(LANES, Q), sds((S, L, LANES), BF), True)],
            scans, (pltpu.VMEM((LANES, Q), F32), pltpu.VMEM((N, I), F32)),
        )
    dpx, dpb, ddt = scans
    hax = shift(dpx[:, :HALO], "seq", -1)
    hab = shift(dpb[:, :HALO], "seq", -1)
    no, ddt = lax.optimization_barrier((no, ddt))
    keep, send_mix, god, gou = pl.pallas_call(
        functools.partial(out_kernel, rank=R),
        grid=grid,
        in_specs=[smem, rows(I, TB), rows(D, TB), rows(D, TB), whole((I, D)), per_seq((LANES, I)),
                  per_seq((LANES, D)), rows(LANES, TB)],
        out_specs=[rows(half, TB), rows(half, TB), per_seq((R, I)), per_seq((R, D))],
        out_shape=[sds((S, L, half), F32), sds((S, L, half), BF), sds((S, R, I), F32), sds((S, R, D), F32)],
        compiler_params=params(2),
        cost_estimate=pl.CostEstimate(
            flops=2 * S * L * I * D, bytes_accessed=S * L * (2 * I + 4 * D), transcendentals=0
        ),
        name="out_proj",
    )(head, no, cotangent, tokens, output_weight, od, ou, blh)
    result = (keep + swap(send_mix).astype(F32)).astype(BF)

    last = L // HALO - 1
    after = lambda s, t: (s, jnp.minimum((t + 1) * per, last), 0)
    kept, send_grad, giz, gix, gid = pl.pallas_call(
        functools.partial(back_kernel, rank=R),
        grid=grid,
        in_specs=[
            smem, rows(I, TB), pl.BlockSpec((1, HALO, I), after), per_seq((HALO, I)),
            rows(2 * N, TB), pl.BlockSpec((1, HALO, 2 * N), after), per_seq((HALO, 2 * N)),
            rows(I, TB), rows(LANES, TB), rows(D, TB), rows(D, TB), whole((1, D)), rows(LANES, TB),
            whole((D, I)), whole((D, I)), whole((D, 2 * N)), whole((D, LANES)),
            per_seq((LANES, D)), per_seq((LANES, I)), per_seq((LANES, I)),
            whole(conv_x.shape), whole(cvb.shape),
        ],
        out_specs=[rows(half, TB), rows(half, TB), per_seq((R, I)), per_seq((R, I)),
                   per_seq((R, D))],
        out_shape=[sds((S, L, half), F32), sds((S, L, half), F32), sds((S, R, I), F32),
                   sds((S, R, I), F32), sds((S, R, D), F32)],
        scratch_shapes=[pltpu.VMEM((TB + HALO, I), F32), pltpu.VMEM((TB + HALO, 2 * N), F32)],
        compiler_params=params(2),
        name="in_back",
    )(head, dpx, dpx, hax, dpb, dpb, hab, dzr, ddt, tokens, cotangent, gain, lrh, wz, wx, wbc, wst, dn, upz, upx,
      conv_x, cvb)

    grad_tokens = (kept + swap(send_grad)).astype(BF)

    if n_head == 2 and I % (LANES * n_seq) == 0 and D % (2 * LANES * n_seq) == 0 and R % 16 == 0 and n_head * I == 2 * D:
        sums_of = exchange(giz, gix, god, gid, gou, adapter_index, head, NA)
        return (result, grad_tokens) + sums_of

    heads_part = jnp.stack([giz, gix, god], 1)
    shared_part = jnp.stack([gid, gou], 1)
    heads_part = lax.all_gather(lax.psum(heads_part, "seq"), "batch")
    shared_part = lax.all_gather(lax.psum(shared_part, ("seq", "head")), "batch")
    index = lax.all_gather(adapter_index, "batch")
    chosen = (index[:, :, None] == jnp.arange(NA)).astype(F32)

    def table(part):
        return jnp.einsum("bsa,bskri->akri", chosen, part, precision=lax.Precision.HIGHEST)

    heads_sum = table(heads_part)
    shared_sum = table(shared_part)
    grad_in_up = jnp.swapaxes(heads_sum[:, :2], 1, 2)
    grad_out_down = jnp.swapaxes(heads_sum[:, 2], 1, 2)
    grad_in_down = jnp.swapaxes(shared_sum[:, 0], 1, 2)
    grad_out_up = shared_sum[:, 1]
    return (result, grad_tokens, grad_in_down, grad_in_up, grad_out_down, grad_out_up)


def solution(mesh):
    in_specs = (
        P("batch", "seq", None),
        P("batch", "seq", None),
        P("batch"),
        P(),
        P(None, None, "head"),
        P(None, None, "head"),
        P(None, "head"),
        P(None, "head"),
        P(None, None, "head"),
        P("head"),
        P("head"),
        P("head"),
        P("head"),
        P("head", None),
        P(),
        P(None, None, None, "head"),
        P(None, "head", None),
        P(),
    )
    out_specs = (
        P("batch", "seq", "head"),
        P("batch", "seq", "head"),
        P(),
        P(None, None, None, "head"),
        P(None, "head", None),
        P(),
    )
    return jax.shard_map(local, mesh=mesh, in_specs=in_specs, out_specs=out_specs, check_vma=False)
```
